32 devices in a mesh: dp: 4 (over z), hid: 2 (over y), dm: 4 (over x, core).
Axes of the slice: x: 2, y: 2, z: 4, core: 2. Of those that a mesh axis runs over, the one named last changes fastest.
Arguments:
- tokens: bfloat16 [16, 1024, 768], P('dp', ('hid', 'dm')), may hold values from -6 to 6
- cluster_ids: int32 [16, 12, 1024], P('dp', None, ('hid', 'dm')), may hold values from 0 to 199, as said below
- first_gain: bfloat16 [768], replicated, may hold values from 0.5 to 1.5
- first_shift: bfloat16 [768], replicated, may hold values from -0.59765625 to 0.59765625
- w_query: bfloat16 [768, 768], replicated, may hold values from -1.5 to 1.5
- b_query: bfloat16 [768], replicated, may hold values from -1.796875 to 1.796875
- w_key: bfloat16 [768, 768], replicated, may hold values from -0.21875 to 0.21875
- w_value: bfloat16 [768, 768], replicated, may hold values from -0.21875 to 0.21875
- b_value: bfloat16 [768], replicated, may hold values from -0.29882812 to 0.29882812
- w_out: bfloat16 [768, 768], replicated, may hold values from -1.75 to 1.75
- b_out: bfloat16 [768], replicated, may hold values from -0.59765625 to 0.59765625
- second_gain: bfloat16 [768], replicated, may hold values from 0.5 to 1.5
- second_shift: bfloat16 [768], replicated, may hold values from -0.59765625 to 0.59765625
- w_up: bfloat16 [768, 3072], P('dm', 'hid'), may hold values from -0.21875 to 0.21875
- b_up: bfloat16 [3072], P('hid'), may hold values from -1.796875 to 1.796875
- w_down: bfloat16 [3072, 768], P('hid', 'dm'), may hold values from -0.109375 to 0.109375
- b_down: bfloat16 [768], replicated, may hold values from -1.1953125 to 1.1953125
- cotangent: bfloat16 [16, 1024, 768], P('dp', ('hid', 'dm')), may hold values from -6 to 6
Outputs:
- output: bfloat16 [16, 1024, 768], P('dp', ('hid', 'dm'))
- grad_tokens: float32 [16, 1024, 768], P('dp', ('hid', 'dm'))
- grad_first_gain: float32 [768], P(('dp', 'hid', 'dm'))
- grad_first_shift: float32 [768], P(('dp', 'hid', 'dm'))
- grad_w_query: float32 [768, 768], P(('dp', 'hid', 'dm'))
- grad_b_query: float32 [768], P(('dp', 'hid', 'dm'))
- grad_w_key: float32 [768, 768], P(('dp', 'hid', 'dm'))
- grad_w_value: float32 [768, 768], P(('dp', 'hid', 'dm'))
- grad_b_value: float32 [768], P(('dp', 'hid', 'dm'))
- grad_w_out: float32 [768, 768], P(('dp', 'hid', 'dm'))
- grad_b_out: float32 [768], P(('dp', 'hid', 'dm'))
- grad_second_gain: float32 [768], P(('dp', 'hid', 'dm'))
- grad_second_shift: float32 [768], P(('dp', 'hid', 'dm'))
- grad_w_up: float32 [768, 3072], P(('dp', 'dm'), 'hid')
- grad_b_up: float32 [3072], P(('dp', 'hid', 'dm'))
- grad_w_down: float32 [3072, 768], P('hid', ('dp', 'dm'))
- grad_b_down: float32 [768], P(('dp', 'hid', 'dm'))
The draws below stay inside these ranges and needn't reach their ends.
Inputs may be any that keep to these rules, and one draw needn't show every extreme that they name: `cluster_ids`: in each sequence all heads use the same number of clusters, one of 25, 100 and 200, and every id below that number occurs in every head; the first sequence uses 200.
All inputs are finite; a program needn't handle non-finite values.
Results may differ from the reference program's by a relative error of at most 0.015.
The reference program's roundings to bfloat16 on the way count: a program that leaves them out, or rounds other values in their place, can miss the bound.
Values may be sent and summed in bfloat16 or wider, within the bound.
No kernel may reach another device: no remote copies, remote signals or barrier semaphores. Data moves between devices by JAX's collectives and lax.ppermute only.
A program may use at most 256 MiB of HBM per device.

```python
import jax
import jax.numpy as jnp
from jax import lax

D = 768
HEADS = 12
HEAD_DIM = 64
FF = 3072
CMAX = 200
LEN = 1024
SEQS = 16


def draw_cluster_ids(key, part):
    count_key, base_key, order_key = jax.random.split(key, 3)
    chosen = jax.random.randint(count_key, (SEQS,), 0, 3)
    chosen = jnp.where(jnp.arange(SEQS) == 0, 2, chosen)
    levels = jnp.array([CMAX // 8, CMAX // 2, CMAX], dtype=jnp.int32)
    clusters = jnp.sum(jnp.where(chosen[:, None] == jnp.arange(3)[None, :], levels[None, :], 0), axis=1)
    random_ids = jax.random.randint(base_key, (SEQS, HEADS, LEN), 0, CMAX) % clusters[:, None, None]
    order_keys = jax.random.split(order_key, SEQS * HEADS)
    orders = jax.vmap(lambda single: jax.random.permutation(single, LEN))(order_keys).reshape(SEQS, HEADS, LEN)
    return jnp.where(orders < clusters[:, None, None], orders, random_ids).astype(jnp.int32)


def block_levels(key, dims, cuts, least, top_value):
    level = 1.0
    for position, shards_of in cuts:
        heights = jax.random.uniform(jax.random.fold_in(jax.random.fold_in(key, 6), position), (shards_of,), jnp.float32, least / len(cuts), top_value / len(cuts))
        level = level * jnp.repeat(jnp.exp(heights), dims[position] // shards_of).reshape((-1,) + (1,) * (len(dims) - 1 - position))
    return level


def centred(own_key, shape, scale, most, cuts=(), kind=jnp.bfloat16):
    values = scale * jax.random.normal(own_key, shape, jnp.float32)
    if cuts:
        values = values * block_levels(own_key, shape, cuts, -0.22, 0.18)
    return jnp.clip(values, -most, most).astype(kind)


def setup_inputs(seed: int = 0) -> dict:
    key_of = jax.random.split(jax.random.key(seed), 19)
    tokens = centred(key_of[0], (SEQS, LEN, D), 1.0, 6.0, ((0, 4), (1, 8)))
    cluster_ids = draw_cluster_ids(jax.random.fold_in(key_of[18], 71), 0)
    first_gain = jnp.clip(1.0 + 0.1 * jax.random.normal(key_of[2], (D,), jnp.float32), 0.5, 1.5).astype(jnp.bfloat16)
    first_shift = centred(key_of[3], (D,), 0.1, 0.59765625)
    w_query = centred(key_of[4], (D, D), (max(1, D * CMAX // (9 * LEN))) ** -0.5, 1.5)
    b_query = centred(key_of[5], (D,), 0.3, 1.796875)
    w_key = centred(key_of[6], (D, D), D ** -0.5, 0.21875)
    w_value = centred(key_of[7], (D, D), D ** -0.5, 0.21875)
    b_value = centred(key_of[8], (D,), 0.05, 0.29882812)
    w_out = centred(key_of[9], (D, D), (D // 64) ** -0.5, 1.75)
    b_out = centred(key_of[10], (D,), 0.1, 0.59765625)
    second_gain = jnp.clip(1.0 + 0.1 * jax.random.normal(key_of[11], (D,), jnp.float32), 0.5, 1.5).astype(jnp.bfloat16)
    second_shift = centred(key_of[12], (D,), 0.1, 0.59765625)
    w_up = centred(key_of[13], (D, FF), D ** -0.5, 0.21875, ((0, 4), (1, 2)))
    b_up = centred(key_of[14], (FF,), 0.3, 1.796875, ((0, 2),))
    w_down = centred(key_of[15], (FF, D), FF ** -0.5, 0.109375, ((0, 2), (1, 4)))
    b_down = centred(key_of[16], (D,), 0.2, 1.1953125)
    cotangent = centred(key_of[17], (SEQS, LEN, D), 1.0, 6.0, ((0, 4), (1, 8)))
    return {"tokens": tokens, "cluster_ids": cluster_ids, "first_gain": first_gain, "first_shift": first_shift, "w_query": w_query, "b_query": b_query, "w_key": w_key, "w_value": w_value, "b_value": b_value, "w_out": w_out, "b_out": b_out, "second_gain": second_gain, "second_shift": second_shift, "w_up": w_up, "b_up": b_up, "w_down": w_down, "b_down": b_down, "cotangent": cotangent}


@jax.custom_vjp
def low(v):
    return lax.optimization_barrier(v.astype(jnp.bfloat16)).astype(jnp.float32)

@jax.custom_vjp
def low_back(v):
    return v

def low_keep(v):
    return (low(v), None)

def low_pass(kept, grad):
    return (grad,)

def back_keep(v):
    return (v, None)

def back_low(kept, grad):
    return (low(grad),)
low.defvjp(low_keep, low_pass)
low_back.defvjp(back_keep, back_low)
EPSILON = 1e-05
ROOT_TWO_PI = 0.7978845608028654
CUBIC_TERM = 0.044715

def layer_norm(values, scale_vec, shift_vec):
    center = values - lax.optimization_barrier(jnp.mean(values, axis=-1, keepdims=True))
    spread = lax.optimization_barrier(jnp.mean(center * center, axis=-1, keepdims=True))
    return center * lax.rsqrt(spread + EPSILON) * scale_vec + shift_vec

def gelu_tanh(values):
    return 0.5 * values * (1.0 + jnp.tanh(ROOT_TWO_PI * (values + CUBIC_TERM * values * values * values)))

def product(left, right):
    return jnp.dot(left, right, precision=lax.Precision.HIGHEST)

def forward(inputs, seq_ids, params):
    first_gain, first_shift, w_query, b_query, w_key, w_value, b_value, w_out, b_out, second_gain, second_shift, w_up, b_up, w_down, b_down = params
    length = inputs.shape[0]
    highest = lax.Precision.HIGHEST
    normed = low(layer_norm(inputs, first_gain, first_shift))
    queries = low_back(low(product(normed, w_query) + b_query))
    key_rows = low_back(low(product(normed, w_key)))
    values = low_back(low(product(normed, w_value) + b_value))
    query_heads = queries.reshape(length, HEADS, HEAD_DIM)
    key_heads = key_rows.reshape(length, HEADS, HEAD_DIM)
    value_heads = values.reshape(length, HEADS, HEAD_DIM)
    member = (seq_ids[:, None, :] == jnp.arange(CMAX, dtype=jnp.int32)[None, :, None]).astype(jnp.float32)
    query_sums = jnp.einsum('hcs,she->che', member, query_heads, precision=highest)
    counts = lax.optimization_barrier(jnp.sum(member, axis=-1))
    centroids = low(query_sums / jnp.maximum(counts, 1.0).T[:, :, None])
    scores = low_back(jnp.einsum('che,she->hcs', centroids, key_heads, precision=highest) * HEAD_DIM ** (-0.5))
    row_max = lax.optimization_barrier(jnp.max(scores, axis=-1, keepdims=True))
    exponent = jnp.exp(scores - row_max)
    prob_rows = exponent / lax.optimization_barrier(jnp.sum(exponent, axis=-1, keepdims=True))
    centroid_out = low(low_back(jnp.einsum('hcs,she->che', low(prob_rows), value_heads, precision=highest)))
    member_out = low_back(jnp.einsum('hcs,che->she', member, centroid_out, precision=highest)).reshape(length, D)
    attention = low_back(product(member_out, w_out) + b_out)
    hidden_sum = inputs + attention
    second = low(layer_norm(hidden_sum, second_gain, second_shift))
    pre_act = low_back(product(second, w_up) + b_up)
    activation = low(gelu_tanh(pre_act))
    branch = low_back(product(activation, w_down) + b_down)
    return hidden_sum + branch

def reference(tokens, cluster_ids, first_gain, first_shift, w_query, b_query, w_key, w_value, b_value, w_out, b_out, second_gain, second_shift, w_up, b_up, w_down, b_down, cotangent):
    params = tuple((element.astype(jnp.float32) for element in (first_gain, first_shift, w_query, b_query, w_key, w_value, b_value, w_out, b_out, second_gain, second_shift, w_up, b_up, w_down, b_down)))
    initial = tuple((jnp.zeros_like(element) for element in params))

    def per_sequence(totals, sequence):
        seq_tokens, seq_ids, seq_grad = sequence

        def apply_layer(inputs, weights):
            return forward(inputs, seq_ids, weights)
        result, pullback = jax.vjp(apply_layer, seq_tokens.astype(jnp.float32), params)
        grad_in, grad_params = pullback(seq_grad.astype(jnp.float32))
        totals = tuple((previous + addition for previous, addition in zip(totals, grad_params)))
        return (totals, (result.astype(jnp.bfloat16), grad_in))
    totals, (output, grad_tokens) = lax.scan(per_sequence, initial, (tokens, cluster_ids, cotangent))
    grad_first_gain, grad_first_shift, grad_w_query, grad_b_query, grad_w_key, grad_w_value, grad_b_value, grad_w_out, grad_b_out, grad_second_gain, grad_second_shift, grad_w_up, grad_b_up, grad_w_down, grad_b_down = totals
    return (output, grad_tokens, grad_first_gain, grad_first_shift, grad_w_query, grad_b_query, grad_w_key, grad_w_value, grad_b_value, grad_w_out, grad_b_out, grad_second_gain, grad_second_shift, grad_w_up, grad_b_up, grad_w_down, grad_b_down)
```

```python
import jax
import jax.numpy as jnp
from jax import lax
from jax.sharding import Mesh
from jax.sharding import PartitionSpec as P

HEADS = 12
HEAD_DIM = 64
FF = 3072
CMAX = 200


EPSILON = 1e-05
ROOT_TWO_PI = 0.7978845608028654
CUBIC_TERM = 0.044715


def combined_all(part, axis, combine):
    gathered = jax.tree.map(lambda a: lax.all_gather(a, axis), part)

    def take(source):
        return jax.tree.map(lambda a: lax.dynamic_index_in_dim(a, source, 0, False), gathered)

    return lax.fori_loop(
        1, lax.axis_size(axis), lambda source, state: combine(state, take(source)), take(0)
    )


def layer_norm(values, scale_vec, shift_vec):
    center = values - jnp.mean(values, axis=-1, keepdims=True)
    spread = jnp.mean(center * center, axis=-1, keepdims=True)
    return center * lax.rsqrt(spread + EPSILON) * scale_vec + shift_vec


def gelu_tanh(values):
    return (
        0.5
        * values
        * (1.0 + jnp.tanh(ROOT_TWO_PI * (values + CUBIC_TERM * values * values * values)))
    )


def matmul(left, right):
    return jnp.dot(left, right, preferred_element_type=jnp.float32)


def contract_rows(left, right):
    return lax.dot_general(
        left, right, (((0,), (0,)), ((), ())), preferred_element_type=jnp.float32
    )


def contract_last(left, right):
    return lax.dot_general(
        left, right, (((1,), (1,)), ((), ())), preferred_element_type=jnp.float32
    )


def merge_parts(earlier, latter):
    early_max, early_sum, early_out = earlier
    late_max, late_sum, late_out = latter
    joint_max = jnp.maximum(early_max, late_max)
    early_scale = jnp.exp(early_max - joint_max)
    late_scale = jnp.exp(late_max - joint_max)
    joint_sum = early_sum * early_scale + late_sum * late_scale
    out_shape = early_out.shape
    head_shape = early_max.shape + (out_shape[-1] // early_max.shape[-1],)
    joint_out = (
        early_out.reshape(head_shape) * early_scale[..., None]
        + late_out.reshape(head_shape) * late_scale[..., None]
    ).reshape(out_shape)
    return (joint_max, joint_sum, joint_out)


def local(
    tokens,
    cluster_ids,
    first_gain,
    first_shift,
    w_query,
    b_query,
    w_key,
    w_value,
    b_value,
    w_out,
    b_out,
    second_gain,
    second_shift,
    w_up,
    b_up,
    w_down,
    b_down,
    cotangent,
):
    groups, seq_rows, model_width = tokens.shape
    row_count = groups * seq_rows
    head_scale = HEAD_DIM ** (-0.5)
    head_shape = (groups, seq_rows, HEADS, HEAD_DIM)
    cent_shape = (groups, CMAX, HEADS, HEAD_DIM)
    first_scale = first_gain.astype(jnp.float32)
    first_bias = first_shift.astype(jnp.float32)
    second_scale = second_gain.astype(jnp.float32)
    second_bias = second_shift.astype(jnp.float32)
    inputs = tokens.reshape(row_count, model_width).astype(jnp.float32)
    normed_low = layer_norm(inputs, first_scale, first_bias).astype(jnp.bfloat16)
    queries = (matmul(normed_low, w_query) + b_query.astype(jnp.float32)).astype(jnp.bfloat16)
    key_rows = matmul(normed_low, w_key).astype(jnp.bfloat16)
    values = (matmul(normed_low, w_value) + b_value.astype(jnp.float32)).astype(jnp.bfloat16)
    query_heads = queries.reshape(head_shape)
    key_heads = key_rows.reshape(head_shape)
    value_heads = values.reshape(head_shape)
    member = cluster_ids[:, :, None, :] == jnp.arange(CMAX, dtype=jnp.int32)[None, None, :, None]
    member_low = member.astype(jnp.bfloat16)
    query_sums = jnp.einsum(
        "ghcs,gshe->gche", member_low, query_heads, preferred_element_type=jnp.float32
    ).reshape(groups, CMAX, model_width)
    counts = jnp.sum(member.astype(jnp.float32), axis=-1)
    query_sums, counts = lax.psum((query_sums, counts), ("hid", "dm"))
    divisor = jnp.transpose(jnp.maximum(counts, 1.0), (0, 2, 1))
    centroid_low = (query_sums.reshape(cent_shape) / divisor[..., None]).astype(jnp.bfloat16)
    scores = (
        jnp.einsum("gche,gshe->ghcs", centroid_low, key_heads, preferred_element_type=jnp.float32)
        * head_scale
    )
    local_max = jnp.max(scores, axis=-1)
    weights = jnp.exp(scores - local_max[..., None])
    local_sum = jnp.sum(weights, axis=-1)
    local_out = jnp.einsum(
        "ghcs,gshe->gche",
        weights.astype(jnp.bfloat16),
        value_heads,
        preferred_element_type=jnp.float32,
    ).reshape(groups, CMAX, model_width)
    merged_max, merged_sum, merged_out = combined_all(
        (jnp.transpose(local_max, (0, 2, 1)), jnp.transpose(local_sum, (0, 2, 1)), local_out),
        ("hid", "dm"),
        merge_parts,
    )
    centroid_out = merged_out.reshape(cent_shape) / merged_sum[..., None]
    log_total = jnp.transpose(merged_max + jnp.log(merged_sum), (0, 2, 1))
    centroid_out_low = centroid_out.astype(jnp.bfloat16)
    member_out = (
        jnp.einsum(
            "ghcs,gche->gshe", member_low, centroid_out_low, preferred_element_type=jnp.float32
        )
        .astype(jnp.bfloat16)
        .reshape(row_count, model_width)
    )
    hidden_sum = inputs + matmul(member_out, w_out) + b_out.astype(jnp.float32)
    second_low = layer_norm(hidden_sum, second_scale, second_bias).astype(jnp.bfloat16)
    up_full, down_full = (
        lax.all_gather(w_up, "dm", axis=0, tiled=True),
        lax.all_gather(w_down, "dm", axis=1, tiled=True),
    )
    grad_out_low = cotangent.reshape(row_count, model_width)
    gathered = lax.all_gather(second_low, "hid", axis=0, tiled=True)
    pre_act = matmul(gathered, up_full) + b_up.astype(jnp.float32)
    activation, gelu_back = jax.vjp(gelu_tanh, pre_act)
    act_low = activation.astype(jnp.bfloat16)
    branch = lax.psum_scatter(matmul(act_low, down_full), "hid", scatter_dimension=0, tiled=True)
    grad_gathered = lax.all_gather(grad_out_low, "hid", axis=0, tiled=True)
    grad_act = contract_last(grad_gathered, down_full)
    grad_pre = gelu_back(grad_act)[0].astype(jnp.bfloat16)
    grad_down_part = contract_rows(act_low, grad_gathered)
    grad_up_part = contract_rows(gathered, grad_pre)
    grad_bias_part = jnp.sum(grad_pre.astype(jnp.float32), axis=0)
    grad_second = lax.psum_scatter(
        contract_last(grad_pre, up_full), "hid", scatter_dimension=0, tiled=True
    )
    output = (hidden_sum + branch + b_down.astype(jnp.float32)).astype(jnp.bfloat16)
    grad_y = grad_out_low.astype(jnp.float32)
    norm_out, second_vjp = jax.vjp(layer_norm, hidden_sum, second_scale, second_bias)
    grad_h_part, grad_second_gain, grad_second_shift = second_vjp(grad_second)
    grad_hidden = grad_y + grad_h_part
    grad_attn_low = grad_hidden.astype(jnp.bfloat16)
    grad_w_out = contract_rows(member_out, grad_attn_low)
    grad_b_out = jnp.sum(grad_attn_low.astype(jnp.float32), axis=0)
    grad_member = contract_last(grad_attn_low, w_out).astype(jnp.bfloat16).reshape(head_shape)
    grad_cent_out = jnp.einsum(
        "ghcs,gshe->gche", member_low, grad_member, preferred_element_type=jnp.float32
    ).reshape(groups, CMAX, model_width)
    grad_cent_out = lax.psum(grad_cent_out, ("hid", "dm"))
    grad_cent_low = grad_cent_out.reshape(cent_shape).astype(jnp.bfloat16)
    prob_rows = jnp.exp(scores - log_total[..., None])
    grad_probs = jnp.einsum(
        "gche,gshe->ghcs", grad_cent_low, value_heads, preferred_element_type=jnp.float32
    )
    delta_rows = lax.psum(jnp.sum(prob_rows * grad_probs, axis=-1), ("hid", "dm"))
    grad_scores = (prob_rows * (grad_probs - delta_rows[..., None])).astype(jnp.bfloat16)
    grad_values = (
        jnp.einsum(
            "ghcs,gche->gshe",
            prob_rows.astype(jnp.bfloat16),
            grad_cent_low,
            preferred_element_type=jnp.float32,
        )
        .astype(jnp.bfloat16)
        .reshape(row_count, model_width)
    )
    grad_keys = (
        (
            jnp.einsum(
                "ghcs,gche->gshe", grad_scores, centroid_low, preferred_element_type=jnp.float32
            )
            * head_scale
        )
        .astype(jnp.bfloat16)
        .reshape(row_count, model_width)
    )
    grad_centroids = (
        jnp.einsum("ghcs,gshe->gche", grad_scores, key_heads, preferred_element_type=jnp.float32)
        * head_scale
    ).reshape(groups, CMAX, model_width)
    grad_centroids = lax.psum(grad_centroids, ("hid", "dm"))
    grad_query_sums = (grad_centroids.reshape(cent_shape) / divisor[..., None]).astype(jnp.bfloat16)
    grad_queries = (
        jnp.einsum(
            "ghcs,gche->gshe", member_low, grad_query_sums, preferred_element_type=jnp.float32
        )
        .astype(jnp.bfloat16)
        .reshape(row_count, model_width)
    )
    grad_w_query = contract_rows(normed_low, grad_queries)
    grad_b_query = jnp.sum(grad_queries.astype(jnp.float32), axis=0)
    grad_w_key = contract_rows(normed_low, grad_keys)
    grad_w_value = contract_rows(normed_low, grad_values)
    grad_b_value = jnp.sum(grad_values.astype(jnp.float32), axis=0)
    grad_normed = (
        contract_last(grad_queries, w_query)
        + contract_last(grad_keys, w_key)
        + contract_last(grad_values, w_value)
    )
    first_out, first_vjp = jax.vjp(layer_norm, inputs, first_scale, first_bias)
    grad_in_part, grad_first_gain, grad_first_shift = first_vjp(grad_normed)
    grad_tokens = (grad_hidden + grad_in_part).reshape(groups, seq_rows, model_width)
    grad_b_down = jnp.sum(grad_y, axis=0)
    bias_full = lax.dynamic_update_slice_in_dim(
        jnp.zeros((FF,), jnp.float32),
        grad_bias_part,
        lax.axis_index("hid") * grad_bias_part.shape[0],
        0,
    )
    grad_w_up, grad_w_down = (
        lax.psum_scatter(grad_up_part, ("dp", "dm"), scatter_dimension=0, tiled=True),
        lax.psum_scatter(grad_down_part, ("dp", "dm"), scatter_dimension=1, tiled=True),
    )
    (
        grad_w_query,
        grad_w_key,
        grad_w_value,
        grad_w_out,
        grad_b_query,
        grad_b_value,
        grad_b_out,
        grad_first_gain,
        grad_first_shift,
        grad_second_gain,
        grad_second_shift,
        grad_b_down,
        grad_b_up,
    ) = (
        lax.psum_scatter(grad_w_query, ("dp", "hid", "dm"), scatter_dimension=0, tiled=True),
        lax.psum_scatter(grad_w_key, ("dp", "hid", "dm"), scatter_dimension=0, tiled=True),
        lax.psum_scatter(grad_w_value, ("dp", "hid", "dm"), scatter_dimension=0, tiled=True),
        lax.psum_scatter(grad_w_out, ("dp", "hid", "dm"), scatter_dimension=0, tiled=True),
        lax.psum_scatter(grad_b_query, ("dp", "hid", "dm"), scatter_dimension=0, tiled=True),
        lax.psum_scatter(grad_b_value, ("dp", "hid", "dm"), scatter_dimension=0, tiled=True),
        lax.psum_scatter(grad_b_out, ("dp", "hid", "dm"), scatter_dimension=0, tiled=True),
        lax.psum_scatter(grad_first_gain, ("dp", "hid", "dm"), scatter_dimension=0, tiled=True),
        lax.psum_scatter(grad_first_shift, ("dp", "hid", "dm"), scatter_dimension=0, tiled=True),
        lax.psum_scatter(grad_second_gain, ("dp", "hid", "dm"), scatter_dimension=0, tiled=True),
        lax.psum_scatter(grad_second_shift, ("dp", "hid", "dm"), scatter_dimension=0, tiled=True),
        lax.psum_scatter(grad_b_down, ("dp", "hid", "dm"), scatter_dimension=0, tiled=True),
        lax.psum_scatter(bias_full, ("dp", "hid", "dm"), scatter_dimension=0, tiled=True),
    )
    return (
        output.reshape(groups, seq_rows, model_width),
        grad_tokens,
        grad_first_gain,
        grad_first_shift,
        grad_w_query,
        grad_b_query,
        grad_w_key,
        grad_w_value,
        grad_b_value,
        grad_w_out,
        grad_b_out,
        grad_second_gain,
        grad_second_shift,
        grad_w_up,
        grad_b_up,
        grad_w_down,
        grad_b_down,
    )


def generic(mesh):
    return jax.shard_map(
        local,
        mesh=mesh,
        in_specs=(
            P("dp", ("hid", "dm"), None),
            P("dp", None, ("hid", "dm")),
            P(),
            P(),
            P(),
            P(),
            P(),
            P(),
            P(),
            P(),
            P(),
            P(),
            P(),
            P("dm", "hid"),
            P("hid"),
            P("hid", "dm"),
            P(),
            P("dp", ("hid", "dm"), None),
        ),
        out_specs=(
            P("dp", ("hid", "dm"), None),
            P("dp", ("hid", "dm"), None),
            P(("dp", "hid", "dm")),
            P(("dp", "hid", "dm")),
            P(("dp", "hid", "dm"), None),
            P(("dp", "hid", "dm")),
            P(("dp", "hid", "dm"), None),
            P(("dp", "hid", "dm"), None),
            P(("dp", "hid", "dm")),
            P(("dp", "hid", "dm"), None),
            P(("dp", "hid", "dm")),
            P(("dp", "hid", "dm")),
            P(("dp", "hid", "dm")),
            P(("dp", "dm"), "hid"),
            P(("dp", "hid", "dm")),
            P("hid", ("dp", "dm")),
            P(("dp", "hid", "dm")),
        ),
        check_vma=False,
    )


BF = jnp.bfloat16
F32 = jnp.float32


def flip(value, axis):
    return lax.ppermute(value, axis, [(0, 1), (1, 0)])


def pick(value, index, dim=0):
    return lax.dynamic_index_in_dim(value, index, dim, False)


def shard_pairs(rounds, step):
    return [((h * rounds + d), ((d ^ step) * 2 + h)) for h in range(2) for d in range(rounds)]


def chip_pairs(step):
    return [(i, i ^ step) for i in range(4)]


def norm_parts(values):
    center = values - jnp.mean(values, axis=-1, keepdims=True)
    spread = jnp.mean(center * center, axis=-1, keepdims=True)
    inverse = lax.rsqrt(spread + EPSILON)
    return center * inverse, inverse


def norm_back(grad, scale, unit, inverse):
    weighted = grad * scale
    return inverse * (
        weighted
        - jnp.mean(weighted, axis=-1, keepdims=True)
        - unit * jnp.mean(weighted * unit, axis=-1, keepdims=True)
    )


def halve(parts, axis, dim, wire):
    own = lax.axis_index(axis)
    away = flip(pick(parts, 1 - own, dim).astype(wire), axis)
    return pick(parts, own, dim) + away.astype(F32)


def chain(parts, axis, wire):
    size = lax.axis_size(axis)
    own = lax.axis_index(axis)
    total = pick(parts, own)
    for up in (True, False):
        moved = None
        place = own if up else size - 1 - own
        pairs = [(i, i + 1) if up else (i + 1, i) for i in range(size - 1)]
        for step in range(1, size):
            share = jnp.minimum(size - step + place, size - 1)
            sent = pick(parts, share if up else size - 1 - share)
            if moved is not None:
                sent = sent + moved
            moved = lax.ppermute(sent.astype(wire), axis, pairs).astype(F32)
        total = total + moved
    return total


def scatter_sum(parts, x_first, wire=BF):
    if x_first:
        parts = halve(parts, "x", 2, wire)
        parts = halve(parts, "y", 1, wire)
    else:
        parts = halve(parts, "y", 1, wire)
        parts = halve(parts, "x", 1, wire)
    return chain(parts, "dp", wire)


def owned(
    tokens,
    cluster_ids,
    first_gain,
    first_shift,
    w_query,
    b_query,
    w_key,
    w_value,
    b_value,
    w_out,
    b_out,
    second_gain,
    second_shift,
    w_up,
    b_up,
    w_down,
    b_down,
    cotangent,
):
    groups, block_rows, width = tokens.shape
    depth = lax.axis_size("dp")
    core = lax.axis_index("c")
    chip = lax.axis_index("y") * 2 + lax.axis_index("x")
    own_rows = groups * block_rows
    heads = HEADS // 2
    half = width // 2
    hidden = w_up.shape[1]
    head_scale = HEAD_DIM ** (-0.5)
    first_scale, first_bias = first_gain.astype(F32), first_shift.astype(F32)
    second_scale, second_bias = second_gain.astype(F32), second_shift.astype(F32)

    def gather_chip(value, dim):
        blocks = [pick(value, chip)]
        for step in range(1, 4):
            blocks.append(lax.ppermute(pick(value, chip ^ step), ("y", "x"), chip_pairs(step)))
        return jnp.concatenate(blocks, axis=dim)

    def return_chip(value):
        blocks = value.reshape(groups, block_rows, width)
        got = [blocks[0]]
        for step in range(1, 4):
            got.append(lax.ppermute(blocks[step], ("y", "x"), chip_pairs(step)))
        got = jnp.stack(got)
        return jnp.stack([pick(got, chip ^ place) for place in range(groups)])

    def both(value):
        return jnp.concatenate([value, flip(value, "c")], axis=0)

    def columns(value):
        return lax.dynamic_slice_in_dim(value, core * half, half, value.ndim - 1)

    inputs_low = gather_chip(tokens, 0)
    ids = gather_chip(cluster_ids, 1)
    ids = jnp.concatenate([ids, flip(ids, "c")], axis=1)
    ids = lax.dynamic_slice_in_dim(ids, core * heads, heads, 0)

    inputs = inputs_low.astype(F32)
    first_unit, first_inverse = norm_parts(inputs)
    normed = both((first_unit * first_scale + first_bias).astype(BF))
    rows = 2 * own_rows

    w_up_in, w_down_in, cot_in, b_up_in, _ = lax.optimization_barrier(
        (w_up, w_down, cotangent, b_up, inputs_low)
    )

    def weight(value, dim):
        got = [lax.ppermute(value, ("y", "x", "c"), shard_pairs(4, step)) for step in range(4)]
        got = jnp.stack(got)
        return jnp.concatenate([pick(got, chip ^ place) for place in range(4)], axis=dim)

    up_full = weight(w_up_in, 0)
    down_full = weight(w_down_in, 1)
    cot_own = gather_chip(cot_in, 0)
    cot_all = both(cot_own)
    bias_up = lax.ppermute(
        b_up_in, ("y", "c"), [(y * 2 + c, c * 2 + y) for y in range(2) for c in range(2)]
    )

    def project(weight_cols, bias):
        result = matmul(normed, weight_cols)
        if bias is not None:
            result = result + columns(bias).astype(F32)
        return result.astype(BF).reshape(rows, heads, HEAD_DIM)

    wq, wk, wv = columns(w_query), columns(w_key), columns(w_value)
    query_heads = project(wq, b_query)
    key_heads = project(wk, None)
    value_heads = project(wv, b_value)
    member = ids[:, None, :] == jnp.arange(CMAX, dtype=jnp.int32)[None, :, None]
    member_low = member.astype(BF)
    query_sums = jnp.einsum("hcs,she->hce", member_low, query_heads, preferred_element_type=F32)
    counts = jnp.sum(member.astype(F32), axis=-1)
    divisor = jnp.maximum(counts, 1.0)[..., None]
    centroid_low = (query_sums / divisor).astype(BF)
    scores = (
        jnp.einsum("hce,she->hcs", centroid_low, key_heads, preferred_element_type=F32) * head_scale
    )
    row_max = jnp.max(scores, axis=-1, keepdims=True)
    powers = jnp.exp(scores - row_max)
    probs = powers / jnp.sum(powers, axis=-1, keepdims=True)
    probs_low = probs.astype(BF)
    centroid_out = jnp.einsum("hcs,she->hce", probs_low, value_heads, preferred_element_type=F32)
    member_half = (
        jnp.einsum(
            "hcs,hce->she", member_low, centroid_out.astype(BF), preferred_element_type=F32
        )
        .astype(BF)
        .reshape(rows, half)
    )
    swapped = flip(member_half, "c")
    swapped = jnp.concatenate([swapped[own_rows:], swapped[:own_rows]], axis=0)
    member_out = jnp.where(
        core == 0,
        jnp.concatenate([member_half, swapped], axis=1),
        jnp.concatenate([swapped, member_half], axis=1),
    )
    hidden_sum = inputs + matmul(member_out[:own_rows], w_out) + b_out.astype(F32)
    second_unit, second_inverse = norm_parts(hidden_sum)
    second = both((second_unit * second_scale + second_bias).astype(BF))

    pre_act = matmul(second, up_full) + bias_up.astype(F32)
    activation, gelu_back = jax.vjp(gelu_tanh, pre_act)
    act_low = activation.astype(BF)
    grad_act = contract_last(cot_all, down_full)
    grad_pre = gelu_back(grad_act)[0].astype(BF)
    second_part = contract_last(grad_pre, up_full)
    grad_second = second_part[:own_rows] + flip(second_part[own_rows:], "c")
    branch_part = matmul(act_low, down_full)
    branch = branch_part[:own_rows] + flip(branch_part[own_rows:], "c")
    output = (hidden_sum + branch + b_down.astype(F32)).astype(BF)
    output = return_chip(output)

    grad_up = contract_rows(second, grad_pre)
    grad_down = contract_rows(cot_all, act_low)
    grad_b_up = jnp.sum(grad_pre.astype(F32), axis=0)

    def hidden_blocks(value):
        split = value.reshape(depth, 2, 2, width // (depth * 4), hidden)
        return jnp.transpose(split, (0, 2, 1, 3, 4))

    swap = [(y * 2 + c, c * 2 + y) for y in range(2) for c in range(2)]
    grad_w_up = lax.ppermute(scatter_sum(hidden_blocks(grad_up), True), ("y", "c"), swap)
    grad_w_down = lax.ppermute(scatter_sum(hidden_blocks(grad_down), False), ("y", "c"), swap).T

    grad_y = cot_own.astype(F32)
    grad_hidden = grad_y + norm_back(grad_second, second_scale, second_unit, second_inverse)
    grad_second_gain = jnp.sum(grad_second * second_unit, axis=0)
    grad_second_shift = jnp.sum(grad_second, axis=0)
    grad_attn_own = grad_hidden.astype(BF)
    grad_attn = both(grad_attn_own)
    grad_out = contract_rows(member_out, columns(grad_attn))
    grad_b_out = jnp.sum(grad_attn_own.astype(F32), axis=0)
    w_out_rows = lax.dynamic_slice_in_dim(w_out, core * half, half, 0)
    grad_member = contract_last(grad_attn, w_out_rows).astype(BF).reshape(rows, heads, HEAD_DIM)
    grad_cent_low = jnp.einsum(
        "hcs,she->hce", member_low, grad_member, preferred_element_type=F32
    ).astype(BF)
    grad_probs = jnp.einsum("hce,she->hcs", grad_cent_low, value_heads, preferred_element_type=F32)
    delta = jnp.sum(probs * grad_probs, axis=-1, keepdims=True)
    grad_scores = (probs * (grad_probs - delta)).astype(BF)
    grad_values = (
        jnp.einsum("hcs,hce->she", probs_low, grad_cent_low, preferred_element_type=F32)
        .astype(BF)
        .reshape(rows, half)
    )
    grad_keys = (
        (
            jnp.einsum("hcs,hce->she", grad_scores, centroid_low, preferred_element_type=F32)
            * head_scale
        )
        .astype(BF)
        .reshape(rows, half)
    )
    grad_centroids = (
        jnp.einsum("hcs,she->hce", grad_scores, key_heads, preferred_element_type=F32) * head_scale
    )
    grad_queries = (
        jnp.einsum(
            "hcs,hce->she",
            member_low,
            (grad_centroids / divisor).astype(BF),
            preferred_element_type=F32,
        )
        .astype(BF)
        .reshape(rows, half)
    )
    normed_part = (
        contract_last(grad_queries, wq)
        + contract_last(grad_keys, wk)
        + contract_last(grad_values, wv)
    )
    grad_normed = normed_part[:own_rows] + flip(normed_part[own_rows:], "c")
    grad_tokens = grad_hidden + norm_back(grad_normed, first_scale, first_unit, first_inverse)
    grad_tokens = return_chip(grad_tokens.astype(BF)).astype(F32)
    grad_first_gain = jnp.sum(grad_normed * first_unit, axis=0)
    grad_first_shift = jnp.sum(grad_normed, axis=0)

    def square_sum(value, x_first):
        split = value.reshape(depth, 2, 2, width // (depth * 4), half)
        total = scatter_sum(split, x_first).reshape(2, -1, half)
        away = flip(pick(total, 1 - core), "c")
        kept = pick(total, core)
        return jnp.where(
            core == 0,
            jnp.concatenate([kept, away], axis=1),
            jnp.concatenate([away, kept], axis=1),
        )

    grad_w_out = square_sum(grad_out, True)
    grad_w_key = square_sum(contract_rows(normed, grad_keys), False)
    grad_w_value = square_sum(contract_rows(normed, grad_values), True)
    grad_w_query = square_sum(contract_rows(normed, grad_queries), False)

    def placed(value, full):
        return lax.dynamic_update_slice_in_dim(
            jnp.zeros((full,), F32), value, core * value.shape[0], 0
        )

    vectors = (
        grad_first_gain,
        grad_first_shift,
        placed(jnp.sum(grad_queries.astype(F32), axis=0), width),
        placed(jnp.sum(grad_values.astype(F32), axis=0), width),
        grad_b_out,
        grad_second_gain,
        grad_second_shift,
        jnp.sum(grad_y, axis=0),
        placed(grad_b_up, 2 * hidden),
    )
    packed = jnp.concatenate([v.reshape(depth, 2, 2, 2, -1) for v in vectors], axis=-1)
    packed = halve(packed, "c", 3, F32)
    packed = scatter_sum(packed, True, F32)
    sizes = [v.shape[0] // (depth * 8) for v in vectors]
    pieces = []
    place = 0
    for size in sizes:
        pieces.append(packed[place : place + size])
        place += size
    return (
        output,
        grad_tokens,
        pieces[0],
        pieces[1],
        grad_w_query,
        pieces[2],
        grad_w_key,
        grad_w_value,
        pieces[3],
        grad_w_out,
        pieces[4],
        pieces[5],
        pieces[6],
        grad_w_up,
        pieces[8],
        grad_w_down,
        pieces[7],
    )


def owning(mesh):
    shape = (mesh.shape["dp"], 2, 2, 2)
    split = Mesh(mesh.devices.reshape(shape), ("dp", "y", "x", "c"))
    rows = ("y", "x", "c")
    whole = ("dp", "y", "x", "c")
    return jax.shard_map(
        owned,
        mesh=split,
        in_specs=(
            P("dp", rows, None),
            P("dp", None, rows),
            *(P(),) * 11,
            P(("x", "c"), "y"),
            P("y"),
            P("y", ("x", "c")),
            P(),
            P("dp", rows, None),
        ),
        out_specs=(
            P("dp", rows, None),
            P("dp", rows, None),
            P(whole),
            P(whole),
            P(whole, None),
            P(whole),
            P(whole, None),
            P(whole, None),
            P(whole),
            P(whole, None),
            P(whole),
            P(whole),
            P(whole),
            P(("dp", "x", "c"), "y"),
            P(whole),
            P("y", ("dp", "x", "c")),
            P(whole),
        ),
        check_vma=False,
    )


def solution(mesh):
    def step(tokens, *rest):
        groups = tokens.shape[0] // mesh.shape["dp"]
        fits = mesh.shape["hid"] == 2 and mesh.shape["dm"] == 4 and groups == 4
        return (owning if fits else generic)(mesh)(tokens, *rest)

    return step
```

```python
import jax
import jax.numpy as jnp
from jax import lax
from jax.sharding import Mesh
from jax.sharding import PartitionSpec as P

HEADS = 12
HEAD_DIM = 64
FF = 3072
CMAX = 200


EPSILON = 1e-05
ROOT_TWO_PI = 0.7978845608028654
CUBIC_TERM = 0.044715


def combined_all(part, axis, combine):
    gathered = jax.tree.map(lambda a: lax.all_gather(a, axis), part)

    def take(source):
        return jax.tree.map(lambda a: lax.dynamic_index_in_dim(a, source, 0, False), gathered)

    return lax.fori_loop(
        1, lax.axis_size(axis), lambda source, state: combine(state, take(source)), take(0)
    )


def layer_norm(values, scale_vec, shift_vec):
    center = values - jnp.mean(values, axis=-1, keepdims=True)
    spread = jnp.mean(center * center, axis=-1, keepdims=True)
    return center * lax.rsqrt(spread + EPSILON) * scale_vec + shift_vec


def gelu_tanh(values):
    return (
        0.5
        * values
        * (1.0 + jnp.tanh(ROOT_TWO_PI * (values + CUBIC_TERM * values * values * values)))
    )


def matmul(left, right):
    return jnp.dot(left, right, preferred_element_type=jnp.float32)


def contract_rows(left, right):
    return lax.dot_general(
        left, right, (((0,), (0,)), ((), ())), preferred_element_type=jnp.float32
    )


def contract_last(left, right):
    return lax.dot_general(
        left, right, (((1,), (1,)), ((), ())), preferred_element_type=jnp.float32
    )


def merge_parts(earlier, latter):
    early_max, early_sum, early_out = earlier
    late_max, late_sum, late_out = latter
    joint_max = jnp.maximum(early_max, late_max)
    early_scale = jnp.exp(early_max - joint_max)
    late_scale = jnp.exp(late_max - joint_max)
    joint_sum = early_sum * early_scale + late_sum * late_scale
    out_shape = early_out.shape
    head_shape = early_max.shape + (out_shape[-1] // early_max.shape[-1],)
    joint_out = (
        early_out.reshape(head_shape) * early_scale[..., None]
        + late_out.reshape(head_shape) * late_scale[..., None]
    ).reshape(out_shape)
    return (joint_max, joint_sum, joint_out)


def local(
    tokens,
    cluster_ids,
    first_gain,
    first_shift,
    w_query,
    b_query,
    w_key,
    w_value,
    b_value,
    w_out,
    b_out,
    second_gain,
    second_shift,
    w_up,
    b_up,
    w_down,
    b_down,
    cotangent,
):
    groups, seq_rows, model_width = tokens.shape
    row_count = groups * seq_rows
    head_scale = HEAD_DIM ** (-0.5)
    head_shape = (groups, seq_rows, HEADS, HEAD_DIM)
    cent_shape = (groups, CMAX, HEADS, HEAD_DIM)
    first_scale = first_gain.astype(jnp.float32)
    first_bias = first_shift.astype(jnp.float32)
    second_scale = second_gain.astype(jnp.float32)
    second_bias = second_shift.astype(jnp.float32)
    inputs = tokens.reshape(row_count, model_width).astype(jnp.float32)
    normed_low = layer_norm(inputs, first_scale, first_bias).astype(jnp.bfloat16)
    queries = (matmul(normed_low, w_query) + b_query.astype(jnp.float32)).astype(jnp.bfloat16)
    key_rows = matmul(normed_low, w_key).astype(jnp.bfloat16)
    values = (matmul(normed_low, w_value) + b_value.astype(jnp.float32)).astype(jnp.bfloat16)
    query_heads = queries.reshape(head_shape)
    key_heads = key_rows.reshape(head_shape)
    value_heads = values.reshape(head_shape)
    member = cluster_ids[:, :, None, :] == jnp.arange(CMAX, dtype=jnp.int32)[None, None, :, None]
    member_low = member.astype(jnp.bfloat16)
    query_sums = jnp.einsum(
        "ghcs,gshe->gche", member_low, query_heads, preferred_element_type=jnp.float32
    ).reshape(groups, CMAX, model_width)
    counts = jnp.sum(member.astype(jnp.float32), axis=-1)
    query_sums, counts = lax.psum((query_sums, counts), ("hid", "dm"))
    divisor = jnp.transpose(jnp.maximum(counts, 1.0), (0, 2, 1))
    centroid_low = (query_sums.reshape(cent_shape) / divisor[..., None]).astype(jnp.bfloat16)
    scores = (
        jnp.einsum("gche,gshe->ghcs", centroid_low, key_heads, preferred_element_type=jnp.float32)
        * head_scale
    )
    local_max = jnp.max(scores, axis=-1)
    weights = jnp.exp(scores - local_max[..., None])
    local_sum = jnp.sum(weights, axis=-1)
    local_out = jnp.einsum(
        "ghcs,gshe->gche",
        weights.astype(jnp.bfloat16),
        value_heads,
        preferred_element_type=jnp.float32,
    ).reshape(groups, CMAX, model_width)
    merged_max, merged_sum, merged_out = combined_all(
        (jnp.transpose(local_max, (0, 2, 1)), jnp.transpose(local_sum, (0, 2, 1)), local_out),
        ("hid", "dm"),
        merge_parts,
    )
    centroid_out = merged_out.reshape(cent_shape) / merged_sum[..., None]
    log_total = jnp.transpose(merged_max + jnp.log(merged_sum), (0, 2, 1))
    centroid_out_low = centroid_out.astype(jnp.bfloat16)
    member_out = (
        jnp.einsum(
            "ghcs,gche->gshe", member_low, centroid_out_low, preferred_element_type=jnp.float32
        )
        .astype(jnp.bfloat16)
        .reshape(row_count, model_width)
    )
    hidden_sum = inputs + matmul(member_out, w_out) + b_out.astype(jnp.float32)
    second_low = layer_norm(hidden_sum, second_scale, second_bias).astype(jnp.bfloat16)
    up_full, down_full = (
        lax.all_gather(w_up, "dm", axis=0, tiled=True),
        lax.all_gather(w_down, "dm", axis=1, tiled=True),
    )
    grad_out_low = cotangent.reshape(row_count, model_width)
    gathered = lax.all_gather(second_low, "hid", axis=0, tiled=True)
    pre_act = matmul(gathered, up_full) + b_up.astype(jnp.float32)
    activation, gelu_back = jax.vjp(gelu_tanh, pre_act)
    act_low = activation.astype(jnp.bfloat16)
    branch = lax.psum_scatter(matmul(act_low, down_full), "hid", scatter_dimension=0, tiled=True)
    grad_gathered = lax.all_gather(grad_out_low, "hid", axis=0, tiled=True)
    grad_act = contract_last(grad_gathered, down_full)
    grad_pre = gelu_back(grad_act)[0].astype(jnp.bfloat16)
    grad_down_part = contract_rows(act_low, grad_gathered)
    grad_up_part = contract_rows(gathered, grad_pre)
    grad_bias_part = jnp.sum(grad_pre.astype(jnp.float32), axis=0)
    grad_second = lax.psum_scatter(
        contract_last(grad_pre, up_full), "hid", scatter_dimension=0, tiled=True
    )
    output = (hidden_sum + branch + b_down.astype(jnp.float32)).astype(jnp.bfloat16)
    grad_y = grad_out_low.astype(jnp.float32)
    norm_out, second_vjp = jax.vjp(layer_norm, hidden_sum, second_scale, second_bias)
    grad_h_part, grad_second_gain, grad_second_shift = second_vjp(grad_second)
    grad_hidden = grad_y + grad_h_part
    grad_attn_low = grad_hidden.astype(jnp.bfloat16)
    grad_w_out = contract_rows(member_out, grad_attn_low)
    grad_b_out = jnp.sum(grad_attn_low.astype(jnp.float32), axis=0)
    grad_member = contract_last(grad_attn_low, w_out).astype(jnp.bfloat16).reshape(head_shape)
    grad_cent_out = jnp.einsum(
        "ghcs,gshe->gche", member_low, grad_member, preferred_element_type=jnp.float32
    ).reshape(groups, CMAX, model_width)
    grad_cent_out = lax.psum(grad_cent_out, ("hid", "dm"))
    grad_cent_low = grad_cent_out.reshape(cent_shape).astype(jnp.bfloat16)
    prob_rows = jnp.exp(scores - log_total[..., None])
    grad_probs = jnp.einsum(
        "gche,gshe->ghcs", grad_cent_low, value_heads, preferred_element_type=jnp.float32
    )
    delta_rows = lax.psum(jnp.sum(prob_rows * grad_probs, axis=-1), ("hid", "dm"))
    grad_scores = (prob_rows * (grad_probs - delta_rows[..., None])).astype(jnp.bfloat16)
    grad_values = (
        jnp.einsum(
            "ghcs,gche->gshe",
            prob_rows.astype(jnp.bfloat16),
            grad_cent_low,
            preferred_element_type=jnp.float32,
        )
        .astype(jnp.bfloat16)
        .reshape(row_count, model_width)
    )
    grad_keys = (
        (
            jnp.einsum(
                "ghcs,gche->gshe", grad_scores, centroid_low, preferred_element_type=jnp.float32
            )
            * head_scale
        )
        .astype(jnp.bfloat16)
        .reshape(row_count, model_width)
    )
    grad_centroids = (
        jnp.einsum("ghcs,gshe->gche", grad_scores, key_heads, preferred_element_type=jnp.float32)
        * head_scale
    ).reshape(groups, CMAX, model_width)
    grad_centroids = lax.psum(grad_centroids, ("hid", "dm"))
    grad_query_sums = (grad_centroids.reshape(cent_shape) / divisor[..., None]).astype(jnp.bfloat16)
    grad_queries = (
        jnp.einsum(
            "ghcs,gche->gshe", member_low, grad_query_sums, preferred_element_type=jnp.float32
        )
        .astype(jnp.bfloat16)
        .reshape(row_count, model_width)
    )
    grad_w_query = contract_rows(normed_low, grad_queries)
    grad_b_query = jnp.sum(grad_queries.astype(jnp.float32), axis=0)
    grad_w_key = contract_rows(normed_low, grad_keys)
    grad_w_value = contract_rows(normed_low, grad_values)
    grad_b_value = jnp.sum(grad_values.astype(jnp.float32), axis=0)
    grad_normed = (
        contract_last(grad_queries, w_query)
        + contract_last(grad_keys, w_key)
        + contract_last(grad_values, w_value)
    )
    first_out, first_vjp = jax.vjp(layer_norm, inputs, first_scale, first_bias)
    grad_in_part, grad_first_gain, grad_first_shift = first_vjp(grad_normed)
    grad_tokens = (grad_hidden + grad_in_part).reshape(groups, seq_rows, model_width)
    grad_b_down = jnp.sum(grad_y, axis=0)
    bias_full = lax.dynamic_update_slice_in_dim(
        jnp.zeros((FF,), jnp.float32),
        grad_bias_part,
        lax.axis_index("hid") * grad_bias_part.shape[0],
        0,
    )
    grad_w_up, grad_w_down = (
        lax.psum_scatter(grad_up_part, ("dp", "dm"), scatter_dimension=0, tiled=True),
        lax.psum_scatter(grad_down_part, ("dp", "dm"), scatter_dimension=1, tiled=True),
    )
    (
        grad_w_query,
        grad_w_key,
        grad_w_value,
        grad_w_out,
        grad_b_query,
        grad_b_value,
        grad_b_out,
        grad_first_gain,
        grad_first_shift,
        grad_second_gain,
        grad_second_shift,
        grad_b_down,
        grad_b_up,
    ) = (
        lax.psum_scatter(grad_w_query, ("dp", "hid", "dm"), scatter_dimension=0, tiled=True),
        lax.psum_scatter(grad_w_key, ("dp", "hid", "dm"), scatter_dimension=0, tiled=True),
        lax.psum_scatter(grad_w_value, ("dp", "hid", "dm"), scatter_dimension=0, tiled=True),
        lax.psum_scatter(grad_w_out, ("dp", "hid", "dm"), scatter_dimension=0, tiled=True),
        lax.psum_scatter(grad_b_query, ("dp", "hid", "dm"), scatter_dimension=0, tiled=True),
        lax.psum_scatter(grad_b_value, ("dp", "hid", "dm"), scatter_dimension=0, tiled=True),
        lax.psum_scatter(grad_b_out, ("dp", "hid", "dm"), scatter_dimension=0, tiled=True),
        lax.psum_scatter(grad_first_gain, ("dp", "hid", "dm"), scatter_dimension=0, tiled=True),
        lax.psum_scatter(grad_first_shift, ("dp", "hid", "dm"), scatter_dimension=0, tiled=True),
        lax.psum_scatter(grad_second_gain, ("dp", "hid", "dm"), scatter_dimension=0, tiled=True),
        lax.psum_scatter(grad_second_shift, ("dp", "hid", "dm"), scatter_dimension=0, tiled=True),
        lax.psum_scatter(grad_b_down, ("dp", "hid", "dm"), scatter_dimension=0, tiled=True),
        lax.psum_scatter(bias_full, ("dp", "hid", "dm"), scatter_dimension=0, tiled=True),
    )
    return (
        output.reshape(groups, seq_rows, model_width),
        grad_tokens,
        grad_first_gain,
        grad_first_shift,
        grad_w_query,
        grad_b_query,
        grad_w_key,
        grad_w_value,
        grad_b_value,
        grad_w_out,
        grad_b_out,
        grad_second_gain,
        grad_second_shift,
        grad_w_up,
        grad_b_up,
        grad_w_down,
        grad_b_down,
    )


def generic(mesh):
    return jax.shard_map(
        local,
        mesh=mesh,
        in_specs=(
            P("dp", ("hid", "dm"), None),
            P("dp", None, ("hid", "dm")),
            P(),
            P(),
            P(),
            P(),
            P(),
            P(),
            P(),
            P(),
            P(),
            P(),
            P(),
            P("dm", "hid"),
            P("hid"),
            P("hid", "dm"),
            P(),
            P("dp", ("hid", "dm"), None),
        ),
        out_specs=(
            P("dp", ("hid", "dm"), None),
            P("dp", ("hid", "dm"), None),
            P(("dp", "hid", "dm")),
            P(("dp", "hid", "dm")),
            P(("dp", "hid", "dm"), None),
            P(("dp", "hid", "dm")),
            P(("dp", "hid", "dm"), None),
            P(("dp", "hid", "dm"), None),
            P(("dp", "hid", "dm")),
            P(("dp", "hid", "dm"), None),
            P(("dp", "hid", "dm")),
            P(("dp", "hid", "dm")),
            P(("dp", "hid", "dm")),
            P(("dp", "dm"), "hid"),
            P(("dp", "hid", "dm")),
            P("hid", ("dp", "dm")),
            P(("dp", "hid", "dm")),
        ),
        check_vma=False,
    )


BF = jnp.bfloat16
F32 = jnp.float32


def flip(value, axis):
    return lax.ppermute(value, axis, [(0, 1), (1, 0)])


def pick(value, index, dim=0):
    return lax.dynamic_index_in_dim(value, index, dim, False)


def chip_pairs(step):
    return [(i, i ^ step) for i in range(4)]


def norm_parts(values):
    center = values - jnp.mean(values, axis=-1, keepdims=True)
    spread = jnp.mean(center * center, axis=-1, keepdims=True)
    inverse = lax.rsqrt(spread + EPSILON)
    return center * inverse, inverse


def norm_back(grad, scale, unit, inverse):
    weighted = grad * scale
    return inverse * (
        weighted
        - jnp.mean(weighted, axis=-1, keepdims=True)
        - unit * jnp.mean(weighted * unit, axis=-1, keepdims=True)
    )


def add_all(parts):
    total = parts[0].astype(F32)
    for part in parts[1:]:
        total = total + part.astype(F32)
    return total


def owned(
    tokens,
    cluster_ids,
    first_gain,
    first_shift,
    w_query,
    b_query,
    w_key,
    w_value,
    b_value,
    w_out,
    b_out,
    second_gain,
    second_shift,
    w_up,
    b_up,
    w_down,
    b_down,
    cotangent,
):
    groups, block_rows, width = tokens.shape
    depth = lax.axis_size("dp")
    layer = lax.axis_index("dp")
    core = lax.axis_index("c")
    at_y, at_x = lax.axis_index("y"), lax.axis_index("x")
    chip = at_y * 2 + at_x
    own_rows = groups * block_rows
    rows = 2 * own_rows
    heads = HEADS // 2
    half = width // 2
    shard_rows, hidden = w_up.shape
    head_scale = HEAD_DIM ** (-0.5)
    first_scale, first_bias = first_gain.astype(F32), first_shift.astype(F32)
    second_scale, second_bias = second_gain.astype(F32), second_shift.astype(F32)
    fence = lax.optimization_barrier

    def over_chips(blocks):
        return [blocks(0)] + [
            lax.ppermute(blocks(step), ("y", "x"), chip_pairs(step)) for step in range(1, 4)
        ]

    def over_layers(parts):
        return add_all(
            [pick(parts, layer)]
            + [
                lax.ppermute(
                    pick(parts, layer ^ step), "dp", [(i, i ^ step) for i in range(depth)]
                )
                for step in range(1, depth)
            ]
        )

    def in_order(blocks):
        got = jnp.stack(blocks)
        return jnp.stack([pick(got, chip ^ place) for place in range(groups)])

    def both(value):
        return jnp.concatenate([value, flip(value, "c")], axis=0)

    def columns(value):
        return lax.dynamic_slice_in_dim(value, core * half, half, value.ndim - 1)

    id_rows = HEADS * block_rows // width
    packed = jnp.concatenate(
        [tokens, cluster_ids.astype(BF).reshape(groups, id_rows, width)], axis=1
    )
    packed = jnp.stack(over_chips(lambda step: pick(packed, chip ^ step)))
    packed = both(packed)
    inputs = packed[:, :block_rows].reshape(rows, width).astype(F32)
    ids = packed[:, block_rows:].reshape(2 * groups, HEADS, block_rows)
    ids = lax.dynamic_slice_in_dim(ids, core * heads, heads, 1).astype(jnp.int32)
    ids = jnp.transpose(ids, (1, 0, 2)).reshape(heads, rows)

    shard = jnp.concatenate(
        [w_up, w_down.T, jnp.broadcast_to(b_up[None], (16, hidden))], axis=0
    )
    shard, cot_in, _ = fence((shard, cotangent, packed))
    got_shards = [
        lax.ppermute(
            shard,
            ("y", "x", "c"),
            [(h * 4 + d, (d ^ step) * 2 + h) for h in range(2) for d in range(4)],
        )
        for step in range(4)
    ]
    cot_own = jnp.concatenate(over_chips(lambda step: pick(cot_in, chip ^ step)), axis=0)
    cot_all = both(cot_own)

    first_unit, first_inverse = norm_parts(inputs)
    normed = (first_unit * first_scale + first_bias).astype(BF)

    def project(weight_cols, bias):
        result = matmul(normed, weight_cols)
        if bias is not None:
            result = result + columns(bias).astype(F32)
        return result.astype(BF).reshape(rows, heads, HEAD_DIM)

    wq, wk, wv = columns(w_query), columns(w_key), columns(w_value)
    query_heads = project(wq, b_query)
    key_heads = project(wk, None)
    value_heads = project(wv, b_value)
    member = ids[:, None, :] == jnp.arange(CMAX, dtype=jnp.int32)[None, :, None]
    member_low = member.astype(BF)
    query_sums = jnp.einsum("hcs,she->hce", member_low, query_heads, preferred_element_type=F32)
    counts = jnp.sum(member.astype(F32), axis=-1)
    divisor = jnp.maximum(counts, 1.0)[..., None]
    centroid_low = (query_sums / divisor).astype(BF)
    scores = (
        jnp.einsum("hce,she->hcs", centroid_low, key_heads, preferred_element_type=F32) * head_scale
    )
    row_max = jnp.max(scores, axis=-1, keepdims=True)
    powers = jnp.exp(scores - row_max)
    probs = powers / jnp.sum(powers, axis=-1, keepdims=True)
    probs_low = probs.astype(BF)
    centroid_out = jnp.einsum("hcs,she->hce", probs_low, value_heads, preferred_element_type=F32)
    member_half = (
        jnp.einsum(
            "hcs,hce->she", member_low, centroid_out.astype(BF), preferred_element_type=F32
        )
        .astype(BF)
        .reshape(rows, half)
    )
    swapped = flip(member_half, "c")
    swapped = jnp.concatenate([swapped[own_rows:], swapped[:own_rows]], axis=0)
    member_out = jnp.where(
        core == 0,
        jnp.concatenate([member_half, swapped], axis=1),
        jnp.concatenate([swapped, member_half], axis=1),
    )
    hidden_sum = inputs[:own_rows] + matmul(member_out[:own_rows], w_out) + b_out.astype(F32)
    second_unit, second_inverse = norm_parts(hidden_sum)
    second = both((second_unit * second_scale + second_bias).astype(BF))

    up_full = in_order([s[:shard_rows] for s in got_shards]).reshape(width, hidden)
    down_full = in_order([s[shard_rows : 2 * shard_rows] for s in got_shards]).reshape(
        width, hidden
    )
    pre_act = matmul(second, up_full) + got_shards[0][2 * shard_rows].astype(F32)
    activation, gelu_back = jax.vjp(gelu_tanh, pre_act)
    act_low = activation.astype(BF)
    grad_act = matmul(cot_all, down_full)
    grad_pre = gelu_back(grad_act)[0].astype(BF)
    second_part = contract_last(grad_pre, up_full)
    grad_second = second_part[:own_rows] + flip(second_part[own_rows:], "c")
    grad_up = contract_rows(second, grad_pre).astype(BF)
    grad_down = contract_rows(cot_all, act_low).astype(BF)
    grad_b_up = jnp.sum(grad_pre.astype(F32), axis=0)

    share = width // (depth * 4)
    wide = [g.reshape(depth, 4, share, hidden) for g in (grad_up, grad_down)]
    sent = []
    for flip_x in range(2):
        for flip_y in range(2):
            place = (at_x ^ flip_x) * 2 + (at_y ^ flip_y)
            piece = jnp.concatenate([pick(g, place, 1) for g in wide], axis=1)
            pairs = [
                (y * 4 + x * 2 + c, c * 4 + (x ^ flip_x) * 2 + (y ^ flip_y))
                for y in range(2)
                for x in range(2)
                for c in range(2)
            ]
            sent.append(lax.ppermute(piece, ("y", "x", "c"), pairs))

    branch_part = contract_last(act_low, down_full)
    branch = branch_part[:own_rows] + flip(branch_part[own_rows:], "c")
    output = (hidden_sum + branch + b_down.astype(F32)).astype(BF)
    output = output.reshape(groups, block_rows, width)
    output = in_order(over_chips(lambda step: output[step]))

    grad_y = cot_own.astype(F32)
    grad_hidden = grad_y + norm_back(grad_second, second_scale, second_unit, second_inverse)
    grad_second_gain = jnp.sum(grad_second * second_unit, axis=0)
    grad_second_shift = jnp.sum(grad_second, axis=0)
    grad_attn_own = grad_hidden.astype(BF)
    grad_attn = both(grad_attn_own)
    grad_out = contract_rows(member_out, columns(grad_attn)).astype(BF)
    grad_b_out = jnp.sum(grad_attn_own.astype(F32), axis=0)
    w_out_rows = lax.dynamic_slice_in_dim(w_out, core * half, half, 0)
    grad_member = contract_last(grad_attn, w_out_rows).astype(BF).reshape(rows, heads, HEAD_DIM)
    grad_cent_low = jnp.einsum(
        "hcs,she->hce", member_low, grad_member, preferred_element_type=F32
    ).astype(BF)
    grad_probs = jnp.einsum("hce,she->hcs", grad_cent_low, value_heads, preferred_element_type=F32)
    delta = jnp.sum(probs * grad_probs, axis=-1, keepdims=True)
    grad_scores = (probs * (grad_probs - delta)).astype(BF)
    grad_values = (
        jnp.einsum("hcs,hce->she", probs_low, grad_cent_low, preferred_element_type=F32)
        .astype(BF)
        .reshape(rows, half)
    )
    grad_keys = (
        (
            jnp.einsum("hcs,hce->she", grad_scores, centroid_low, preferred_element_type=F32)
            * head_scale
        )
        .astype(BF)
        .reshape(rows, half)
    )
    grad_centroids = (
        jnp.einsum("hcs,she->hce", grad_scores, key_heads, preferred_element_type=F32) * head_scale
    )
    grad_queries = (
        jnp.einsum(
            "hcs,hce->she",
            member_low,
            (grad_centroids / divisor).astype(BF),
            preferred_element_type=F32,
        )
        .astype(BF)
        .reshape(rows, half)
    )
    squares = jnp.concatenate(
        [
            contract_rows(normed, grad_queries).astype(BF),
            contract_rows(normed, grad_keys).astype(BF),
            contract_rows(normed, grad_values).astype(BF),
            grad_out,
        ],
        axis=1,
    ).reshape(depth, 4, share, 4 * half)
    square_parts = over_chips(lambda step: pick(squares, chip ^ step, 1))
    sent, square_parts = fence((sent, square_parts))
    wide_sum = over_layers(add_all(sent).astype(BF))
    grad_w_up = wide_sum[:share]
    grad_w_down = wide_sum[share:].T

    normed_part = (
        contract_last(grad_queries, wq)
        + contract_last(grad_keys, wk)
        + contract_last(grad_values, wv)
    )
    grad_normed = normed_part[:own_rows] + flip(normed_part[own_rows:], "c")
    own_unit = first_unit[:own_rows]
    grad_tokens = grad_hidden + norm_back(
        grad_normed, first_scale, own_unit, first_inverse[:own_rows]
    )

    def placed(value, full):
        return lax.dynamic_update_slice_in_dim(
            jnp.zeros((full,), F32), value, core * value.shape[0], 0
        )

    vectors = (
        jnp.sum(grad_normed * own_unit, axis=0),
        jnp.sum(grad_normed, axis=0),
        placed(jnp.sum(grad_queries.astype(F32), axis=0), width),
        placed(jnp.sum(grad_values.astype(F32), axis=0), width),
        grad_b_out,
        grad_second_gain,
        grad_second_shift,
        jnp.sum(grad_y, axis=0),
        placed(grad_b_up, 2 * hidden),
    )
    sizes = [v.shape[0] // (depth * 8) for v in vectors]
    line = 2 * sum(sizes)
    lines = jnp.concatenate([v.reshape(depth, 4, 2, -1) for v in vectors], axis=-1)
    lines = lines.reshape(depth, 4, line).astype(BF)
    vector_rows = depth * line // width
    blocks = grad_tokens.astype(BF).reshape(groups, block_rows, width)
    last = over_chips(
        lambda step: jnp.concatenate(
            [blocks[step], pick(lines, chip ^ step, 1).reshape(vector_rows, width)], axis=0
        )
    )
    grad_tokens = in_order([part[:block_rows] for part in last]).astype(F32)
    line_sum = add_all([part[block_rows:] for part in last]).reshape(depth, line)
    line_sum = jnp.pad(line_sum, ((0, 0), (0, 4 * half - line)))[:, None]
    total = over_layers(
        jnp.concatenate([add_all(square_parts), line_sum], axis=1).astype(BF)
    )
    tile = share // 2
    squared = total[:share].reshape(2, tile, 4 * half)
    piece = total[share, :line].reshape(2, line // 2)
    piece_rows = jnp.pad(piece, ((0, 0), (0, 4 * half - line // 2)))[:, None]
    traded = jnp.concatenate([squared, piece_rows], axis=1)
    away = flip(pick(traded, 1 - core), "c")
    kept = pick(traded, core)
    line_own = (kept[tile] + away[tile])[: line // 2]
    kept, away = kept[:tile].reshape(tile, 4, half), away[:tile].reshape(tile, 4, half)
    full = jnp.where(
        core == 0,
        jnp.concatenate([kept, away], axis=2),
        jnp.concatenate([away, kept], axis=2),
    )
    pieces = []
    place = 0
    for size in sizes:
        pieces.append(line_own[place : place + size])
        place += size
    return (
        output,
        grad_tokens,
        pieces[0],
        pieces[1],
        full[:, 0],
        pieces[2],
        full[:, 1],
        full[:, 2],
        pieces[3],
        full[:, 3],
        pieces[4],
        pieces[5],
        pieces[6],
        grad_w_up,
        pieces[8],
        grad_w_down,
        pieces[7],
    )


def owning(mesh):
    shape = (mesh.shape["dp"], 2, 2, 2)
    split = Mesh(mesh.devices.reshape(shape), ("dp", "y", "x", "c"))
    rows = ("y", "x", "c")
    whole = ("dp", "y", "x", "c")
    return jax.shard_map(
        owned,
        mesh=split,
        in_specs=(
            P("dp", rows, None),
            P("dp", None, rows),
            *(P(),) * 11,
            P(("x", "c"), "y"),
            P("y"),
            P("y", ("x", "c")),
            P(),
            P("dp", rows, None),
        ),
        out_specs=(
            P("dp", rows, None),
            P("dp", rows, None),
            P(whole),
            P(whole),
            P(whole, None),
            P(whole),
            P(whole, None),
            P(whole, None),
            P(whole),
            P(whole, None),
            P(whole),
            P(whole),
            P(whole),
            P(("dp", "x", "c"), "y"),
            P(whole),
            P("y", ("dp", "x", "c")),
            P(whole),
        ),
        check_vma=False,
    )


def solution(mesh):
    def step(tokens, *rest):
        groups = tokens.shape[0] // mesh.shape["dp"]
        fits = mesh.shape["hid"] == 2 and mesh.shape["dm"] == 4 and groups == 4
        return (owning if fits else generic)(mesh)(tokens, *rest)

    return step
```

```python
import jax
import jax.numpy as jnp
from jax import lax
from jax.sharding import Mesh
from jax.sharding import PartitionSpec as P

HEADS = 12
HEAD_DIM = 64
FF = 3072
CMAX = 200


EPSILON = 1e-05
ROOT_TWO_PI = 0.7978845608028654
CUBIC_TERM = 0.044715


def combined_all(part, axis, combine):
    gathered = jax.tree.map(lambda a: lax.all_gather(a, axis), part)

    def take(source):
        return jax.tree.map(lambda a: lax.dynamic_index_in_dim(a, source, 0, False), gathered)

    return lax.fori_loop(
        1, lax.axis_size(axis), lambda source, state: combine(state, take(source)), take(0)
    )


def layer_norm(values, scale_vec, shift_vec):
    center = values - jnp.mean(values, axis=-1, keepdims=True)
    spread = jnp.mean(center * center, axis=-1, keepdims=True)
    return center * lax.rsqrt(spread + EPSILON) * scale_vec + shift_vec


def gelu_tanh(values):
    return (
        0.5
        * values
        * (1.0 + jnp.tanh(ROOT_TWO_PI * (values + CUBIC_TERM * values * values * values)))
    )


def matmul(left, right):
    return jnp.dot(left, right, preferred_element_type=jnp.float32)


def contract_rows(left, right):
    return lax.dot_general(
        left, right, (((0,), (0,)), ((), ())), preferred_element_type=jnp.float32
    )


def contract_last(left, right):
    return lax.dot_general(
        left, right, (((1,), (1,)), ((), ())), preferred_element_type=jnp.float32
    )


def merge_parts(earlier, latter):
    early_max, early_sum, early_out = earlier
    late_max, late_sum, late_out = latter
    joint_max = jnp.maximum(early_max, late_max)
    early_scale = jnp.exp(early_max - joint_max)
    late_scale = jnp.exp(late_max - joint_max)
    joint_sum = early_sum * early_scale + late_sum * late_scale
    out_shape = early_out.shape
    head_shape = early_max.shape + (out_shape[-1] // early_max.shape[-1],)
    joint_out = (
        early_out.reshape(head_shape) * early_scale[..., None]
        + late_out.reshape(head_shape) * late_scale[..., None]
    ).reshape(out_shape)
    return (joint_max, joint_sum, joint_out)


def local(
    tokens,
    cluster_ids,
    first_gain,
    first_shift,
    w_query,
    b_query,
    w_key,
    w_value,
    b_value,
    w_out,
    b_out,
    second_gain,
    second_shift,
    w_up,
    b_up,
    w_down,
    b_down,
    cotangent,
):
    groups, seq_rows, model_width = tokens.shape
    row_count = groups * seq_rows
    head_scale = HEAD_DIM ** (-0.5)
    head_shape = (groups, seq_rows, HEADS, HEAD_DIM)
    cent_shape = (groups, CMAX, HEADS, HEAD_DIM)
    first_scale = first_gain.astype(jnp.float32)
    first_bias = first_shift.astype(jnp.float32)
    second_scale = second_gain.astype(jnp.float32)
    second_bias = second_shift.astype(jnp.float32)
    inputs = tokens.reshape(row_count, model_width).astype(jnp.float32)
    normed_low = layer_norm(inputs, first_scale, first_bias).astype(jnp.bfloat16)
    queries = (matmul(normed_low, w_query) + b_query.astype(jnp.float32)).astype(jnp.bfloat16)
    key_rows = matmul(normed_low, w_key).astype(jnp.bfloat16)
    values = (matmul(normed_low, w_value) + b_value.astype(jnp.float32)).astype(jnp.bfloat16)
    query_heads = queries.reshape(head_shape)
    key_heads = key_rows.reshape(head_shape)
    value_heads = values.reshape(head_shape)
    member = cluster_ids[:, :, None, :] == jnp.arange(CMAX, dtype=jnp.int32)[None, None, :, None]
    member_low = member.astype(jnp.bfloat16)
    query_sums = jnp.einsum(
        "ghcs,gshe->gche", member_low, query_heads, preferred_element_type=jnp.float32
    ).reshape(groups, CMAX, model_width)
    counts = jnp.sum(member.astype(jnp.float32), axis=-1)
    query_sums, counts = lax.psum((query_sums, counts), ("hid", "dm"))
    divisor = jnp.transpose(jnp.maximum(counts, 1.0), (0, 2, 1))
    centroid_low = (query_sums.reshape(cent_shape) / divisor[..., None]).astype(jnp.bfloat16)
    scores = (
        jnp.einsum("gche,gshe->ghcs", centroid_low, key_heads, preferred_element_type=jnp.float32)
        * head_scale
    )
    local_max = jnp.max(scores, axis=-1)
    weights = jnp.exp(scores - local_max[..., None])
    local_sum = jnp.sum(weights, axis=-1)
    local_out = jnp.einsum(
        "ghcs,gshe->gche",
        weights.astype(jnp.bfloat16),
        value_heads,
        preferred_element_type=jnp.float32,
    ).reshape(groups, CMAX, model_width)
    merged_max, merged_sum, merged_out = combined_all(
        (jnp.transpose(local_max, (0, 2, 1)), jnp.transpose(local_sum, (0, 2, 1)), local_out),
        ("hid", "dm"),
        merge_parts,
    )
    centroid_out = merged_out.reshape(cent_shape) / merged_sum[..., None]
    log_total = jnp.transpose(merged_max + jnp.log(merged_sum), (0, 2, 1))
    centroid_out_low = centroid_out.astype(jnp.bfloat16)
    member_out = (
        jnp.einsum(
            "ghcs,gche->gshe", member_low, centroid_out_low, preferred_element_type=jnp.float32
        )
        .astype(jnp.bfloat16)
        .reshape(row_count, model_width)
    )
    hidden_sum = inputs + matmul(member_out, w_out) + b_out.astype(jnp.float32)
    second_low = layer_norm(hidden_sum, second_scale, second_bias).astype(jnp.bfloat16)
    up_full, down_full = (
        lax.all_gather(w_up, "dm", axis=0, tiled=True),
        lax.all_gather(w_down, "dm", axis=1, tiled=True),
    )
    grad_out_low = cotangent.reshape(row_count, model_width)
    gathered = lax.all_gather(second_low, "hid", axis=0, tiled=True)
    pre_act = matmul(gathered, up_full) + b_up.astype(jnp.float32)
    activation, gelu_back = jax.vjp(gelu_tanh, pre_act)
    act_low = activation.astype(jnp.bfloat16)
    branch = lax.psum_scatter(matmul(act_low, down_full), "hid", scatter_dimension=0, tiled=True)
    grad_gathered = lax.all_gather(grad_out_low, "hid", axis=0, tiled=True)
    grad_act = contract_last(grad_gathered, down_full)
    grad_pre = gelu_back(grad_act)[0].astype(jnp.bfloat16)
    grad_down_part = contract_rows(act_low, grad_gathered)
    grad_up_part = contract_rows(gathered, grad_pre)
    grad_bias_part = jnp.sum(grad_pre.astype(jnp.float32), axis=0)
    grad_second = lax.psum_scatter(
        contract_last(grad_pre, up_full), "hid", scatter_dimension=0, tiled=True
    )
    output = (hidden_sum + branch + b_down.astype(jnp.float32)).astype(jnp.bfloat16)
    grad_y = grad_out_low.astype(jnp.float32)
    norm_out, second_vjp = jax.vjp(layer_norm, hidden_sum, second_scale, second_bias)
    grad_h_part, grad_second_gain, grad_second_shift = second_vjp(grad_second)
    grad_hidden = grad_y + grad_h_part
    grad_attn_low = grad_hidden.astype(jnp.bfloat16)
    grad_w_out = contract_rows(member_out, grad_attn_low)
    grad_b_out = jnp.sum(grad_attn_low.astype(jnp.float32), axis=0)
    grad_member = contract_last(grad_attn_low, w_out).astype(jnp.bfloat16).reshape(head_shape)
    grad_cent_out = jnp.einsum(
        "ghcs,gshe->gche", member_low, grad_member, preferred_element_type=jnp.float32
    ).reshape(groups, CMAX, model_width)
    grad_cent_out = lax.psum(grad_cent_out, ("hid", "dm"))
    grad_cent_low = grad_cent_out.reshape(cent_shape).astype(jnp.bfloat16)
    prob_rows = jnp.exp(scores - log_total[..., None])
    grad_probs = jnp.einsum(
        "gche,gshe->ghcs", grad_cent_low, value_heads, preferred_element_type=jnp.float32
    )
    delta_rows = lax.psum(jnp.sum(prob_rows * grad_probs, axis=-1), ("hid", "dm"))
    grad_scores = (prob_rows * (grad_probs - delta_rows[..., None])).astype(jnp.bfloat16)
    grad_values = (
        jnp.einsum(
            "ghcs,gche->gshe",
            prob_rows.astype(jnp.bfloat16),
            grad_cent_low,
            preferred_element_type=jnp.float32,
        )
        .astype(jnp.bfloat16)
        .reshape(row_count, model_width)
    )
    grad_keys = (
        (
            jnp.einsum(
                "ghcs,gche->gshe", grad_scores, centroid_low, preferred_element_type=jnp.float32
            )
            * head_scale
        )
        .astype(jnp.bfloat16)
        .reshape(row_count, model_width)
    )
    grad_centroids = (
        jnp.einsum("ghcs,gshe->gche", grad_scores, key_heads, preferred_element_type=jnp.float32)
        * head_scale
    ).reshape(groups, CMAX, model_width)
    grad_centroids = lax.psum(grad_centroids, ("hid", "dm"))
    grad_query_sums = (grad_centroids.reshape(cent_shape) / divisor[..., None]).astype(jnp.bfloat16)
    grad_queries = (
        jnp.einsum(
            "ghcs,gche->gshe", member_low, grad_query_sums, preferred_element_type=jnp.float32
        )
        .astype(jnp.bfloat16)
        .reshape(row_count, model_width)
    )
    grad_w_query = contract_rows(normed_low, grad_queries)
    grad_b_query = jnp.sum(grad_queries.astype(jnp.float32), axis=0)
    grad_w_key = contract_rows(normed_low, grad_keys)
    grad_w_value = contract_rows(normed_low, grad_values)
    grad_b_value = jnp.sum(grad_values.astype(jnp.float32), axis=0)
    grad_normed = (
        contract_last(grad_queries, w_query)
        + contract_last(grad_keys, w_key)
        + contract_last(grad_values, w_value)
    )
    first_out, first_vjp = jax.vjp(layer_norm, inputs, first_scale, first_bias)
    grad_in_part, grad_first_gain, grad_first_shift = first_vjp(grad_normed)
    grad_tokens = (grad_hidden + grad_in_part).reshape(groups, seq_rows, model_width)
    grad_b_down = jnp.sum(grad_y, axis=0)
    bias_full = lax.dynamic_update_slice_in_dim(
        jnp.zeros((FF,), jnp.float32),
        grad_bias_part,
        lax.axis_index("hid") * grad_bias_part.shape[0],
        0,
    )
    grad_w_up, grad_w_down = (
        lax.psum_scatter(grad_up_part, ("dp", "dm"), scatter_dimension=0, tiled=True),
        lax.psum_scatter(grad_down_part, ("dp", "dm"), scatter_dimension=1, tiled=True),
    )
    (
        grad_w_query,
        grad_w_key,
        grad_w_value,
        grad_w_out,
        grad_b_query,
        grad_b_value,
        grad_b_out,
        grad_first_gain,
        grad_first_shift,
        grad_second_gain,
        grad_second_shift,
        grad_b_down,
        grad_b_up,
    ) = (
        lax.psum_scatter(grad_w_query, ("dp", "hid", "dm"), scatter_dimension=0, tiled=True),
        lax.psum_scatter(grad_w_key, ("dp", "hid", "dm"), scatter_dimension=0, tiled=True),
        lax.psum_scatter(grad_w_value, ("dp", "hid", "dm"), scatter_dimension=0, tiled=True),
        lax.psum_scatter(grad_w_out, ("dp", "hid", "dm"), scatter_dimension=0, tiled=True),
        lax.psum_scatter(grad_b_query, ("dp", "hid", "dm"), scatter_dimension=0, tiled=True),
        lax.psum_scatter(grad_b_value, ("dp", "hid", "dm"), scatter_dimension=0, tiled=True),
        lax.psum_scatter(grad_b_out, ("dp", "hid", "dm"), scatter_dimension=0, tiled=True),
        lax.psum_scatter(grad_first_gain, ("dp", "hid", "dm"), scatter_dimension=0, tiled=True),
        lax.psum_scatter(grad_first_shift, ("dp", "hid", "dm"), scatter_dimension=0, tiled=True),
        lax.psum_scatter(grad_second_gain, ("dp", "hid", "dm"), scatter_dimension=0, tiled=True),
        lax.psum_scatter(grad_second_shift, ("dp", "hid", "dm"), scatter_dimension=0, tiled=True),
        lax.psum_scatter(grad_b_down, ("dp", "hid", "dm"), scatter_dimension=0, tiled=True),
        lax.psum_scatter(bias_full, ("dp", "hid", "dm"), scatter_dimension=0, tiled=True),
    )
    return (
        output.reshape(groups, seq_rows, model_width),
        grad_tokens,
        grad_first_gain,
        grad_first_shift,
        grad_w_query,
        grad_b_query,
        grad_w_key,
        grad_w_value,
        grad_b_value,
        grad_w_out,
        grad_b_out,
        grad_second_gain,
        grad_second_shift,
        grad_w_up,
        grad_b_up,
        grad_w_down,
        grad_b_down,
    )


def generic(mesh):
    return jax.shard_map(
        local,
        mesh=mesh,
        in_specs=(
            P("dp", ("hid", "dm"), None),
            P("dp", None, ("hid", "dm")),
            P(),
            P(),
            P(),
            P(),
            P(),
            P(),
            P(),
            P(),
            P(),
            P(),
            P(),
            P("dm", "hid"),
            P("hid"),
            P("hid", "dm"),
            P(),
            P("dp", ("hid", "dm"), None),
        ),
        out_specs=(
            P("dp", ("hid", "dm"), None),
            P("dp", ("hid", "dm"), None),
            P(("dp", "hid", "dm")),
            P(("dp", "hid", "dm")),
            P(("dp", "hid", "dm"), None),
            P(("dp", "hid", "dm")),
            P(("dp", "hid", "dm"), None),
            P(("dp", "hid", "dm"), None),
            P(("dp", "hid", "dm")),
            P(("dp", "hid", "dm"), None),
            P(("dp", "hid", "dm")),
            P(("dp", "hid", "dm")),
            P(("dp", "hid", "dm")),
            P(("dp", "dm"), "hid"),
            P(("dp", "hid", "dm")),
            P("hid", ("dp", "dm")),
            P(("dp", "hid", "dm")),
        ),
        check_vma=False,
    )


BF = jnp.bfloat16
F32 = jnp.float32


def flip(value, axis):
    return lax.ppermute(value, axis, [(0, 1), (1, 0)])


def pick(value, index, dim=0):
    return lax.dynamic_index_in_dim(value, index, dim, False)


def chip_pairs(step):
    return [(i, i ^ step) for i in range(4)]


def norm_parts(values):
    center = values - jnp.mean(values, axis=-1, keepdims=True)
    spread = jnp.mean(center * center, axis=-1, keepdims=True)
    inverse = lax.rsqrt(spread + EPSILON)
    return center * inverse, inverse


def norm_back(grad, scale, unit, inverse):
    weighted = grad * scale
    return inverse * (
        weighted
        - jnp.mean(weighted, axis=-1, keepdims=True)
        - unit * jnp.mean(weighted * unit, axis=-1, keepdims=True)
    )


def add_all(parts):
    total = parts[0].astype(F32)
    for part in parts[1:]:
        total = total + part.astype(F32)
    return total


def owned(
    tokens,
    cluster_ids,
    first_gain,
    first_shift,
    w_query,
    b_query,
    w_key,
    w_value,
    b_value,
    w_out,
    b_out,
    second_gain,
    second_shift,
    w_up,
    b_up,
    w_down,
    b_down,
    cotangent,
):
    groups, block_rows, width = tokens.shape
    depth = lax.axis_size("dp")
    layer = lax.axis_index("dp")
    core = lax.axis_index("c")
    at_y, at_x = lax.axis_index("y"), lax.axis_index("x")
    chip = at_y * 2 + at_x
    own_rows = groups * block_rows
    rows = 2 * own_rows
    heads = HEADS // 2
    half = width // 2
    shard_rows, hidden = w_up.shape
    head_scale = HEAD_DIM ** (-0.5)
    first_scale, first_bias = first_gain.astype(F32), first_shift.astype(F32)
    second_scale, second_bias = second_gain.astype(F32), second_shift.astype(F32)
    fence = lax.optimization_barrier

    def over_chips(blocks):
        return [blocks(0)] + [
            lax.ppermute(blocks(step), ("y", "x"), chip_pairs(step)) for step in range(1, 4)
        ]

    def over_layers(parts):
        return add_all(
            [pick(parts, layer)]
            + [
                lax.ppermute(
                    pick(parts, layer ^ step), "dp", [(i, i ^ step) for i in range(depth)]
                )
                for step in range(1, depth)
            ]
        )

    def in_order(blocks):
        got = jnp.stack(blocks)
        return jnp.stack([pick(got, chip ^ place) for place in range(groups)])

    def both(value):
        return jnp.concatenate([value, flip(value, "c")], axis=0)

    def columns(value):
        return lax.dynamic_slice_in_dim(value, core * half, half, value.ndim - 1)

    inputs = both(jnp.stack(over_chips(lambda step: pick(tokens, chip ^ step))))
    ids = both(jnp.stack(over_chips(lambda step: pick(cluster_ids, chip ^ step))))
    shard_up, shard_down, inputs, cot_in = fence(
        (
            jnp.concatenate([w_up, jnp.broadcast_to(b_up[None], (16, hidden))], axis=0),
            w_down.T,
            inputs,
            cotangent,
        )
    )
    inputs = inputs.reshape(rows, width).astype(F32)
    ids = lax.dynamic_slice_in_dim(ids, core * heads, heads, 1)
    ids = jnp.transpose(ids, (1, 0, 2)).reshape(heads, rows)

    up_pair = jnp.stack([shard_up, flip(shard_up, "x")])
    down_pair = jnp.stack([shard_down, flip(shard_down, "y")])

    first_unit, first_inverse = norm_parts(inputs)
    normed = (first_unit * first_scale + first_bias).astype(BF)

    def project(weight_cols, bias):
        result = matmul(normed, weight_cols)
        if bias is not None:
            result = result + columns(bias).astype(F32)
        return result.astype(BF).reshape(rows, heads, HEAD_DIM)

    wq, wk, wv = columns(w_query), columns(w_key), columns(w_value)
    query_heads = project(wq, b_query)
    key_heads = project(wk, None)
    value_heads = project(wv, b_value)
    member = ids[:, None, :] == jnp.arange(CMAX, dtype=jnp.int32)[None, :, None]
    member_low = member.astype(BF)
    query_sums = jnp.einsum("hcs,she->hce", member_low, query_heads, preferred_element_type=F32)
    counts = jnp.sum(member.astype(F32), axis=-1)
    divisor = jnp.maximum(counts, 1.0)[..., None]
    centroid_low = (query_sums / divisor).astype(BF)
    scores = (
        jnp.einsum("hce,she->hcs", centroid_low, key_heads, preferred_element_type=F32) * head_scale
    )
    up_pair, down_pair, scores = fence((up_pair, down_pair, scores))
    up_away = flip(up_pair, "y")
    down_away = flip(down_pair, "x")
    cot_own = jnp.concatenate(over_chips(lambda step: pick(cot_in, chip ^ step)), axis=0)
    row_max = jnp.max(scores, axis=-1, keepdims=True)
    powers = jnp.exp(scores - row_max)
    probs = powers / jnp.sum(powers, axis=-1, keepdims=True)
    probs_low = probs.astype(BF)
    centroid_out = jnp.einsum("hcs,she->hce", probs_low, value_heads, preferred_element_type=F32)
    member_half = (
        jnp.einsum(
            "hcs,hce->she", member_low, centroid_out.astype(BF), preferred_element_type=F32
        )
        .astype(BF)
        .reshape(rows, half)
    )
    swapped = flip(member_half, "c")
    swapped = jnp.concatenate([swapped[own_rows:], swapped[:own_rows]], axis=0)
    member_out = jnp.where(
        core == 0,
        jnp.concatenate([member_half, swapped], axis=1),
        jnp.concatenate([swapped, member_half], axis=1),
    )
    hidden_sum = inputs[:own_rows] + matmul(member_out[:own_rows], w_out) + b_out.astype(F32)
    second_unit, second_inverse = norm_parts(hidden_sum)
    second = both((second_unit * second_scale + second_bias).astype(BF))

    same = at_y == core

    def assemble(own_y, away_y):
        kept = jnp.where(same, own_y, away_y)
        got = flip(jnp.where(same, away_y, own_y), "c")
        parts = [[pick(v, at_x ^ x)[:shard_rows] for x in range(2)] for v in (kept, got)]
        ordered = [
            jnp.where(core == c, parts[0][x], parts[1][x]) for x in range(2) for c in range(2)
        ]
        return jnp.concatenate(ordered, axis=0), kept

    up_full, up_kept = assemble(up_pair, up_away)
    down_full, _ = assemble(
        jnp.stack([down_pair[0], down_away[0]]), jnp.stack([down_pair[1], down_away[1]])
    )
    cot_all = both(cot_own)
    pre_act = matmul(second, up_full) + up_kept[0, shard_rows].astype(F32)
    activation, gelu_back = jax.vjp(gelu_tanh, pre_act)
    act_low = activation.astype(BF)
    grad_act = matmul(cot_all, down_full)
    grad_pre = gelu_back(grad_act)[0].astype(BF)
    grad_up = contract_rows(second, grad_pre).astype(BF)
    grad_down = contract_rows(cot_all, act_low).astype(BF)
    grad_b_up = jnp.sum(grad_pre.astype(F32), axis=0)

    def halve(parts, axis, dim):
        own = at_x if axis == "x" else at_y
        return pick(parts, own, dim), flip(pick(parts, 1 - own, dim), axis)

    def joined(pair):
        return (pair[0].astype(F32) + pair[1].astype(F32)).astype(BF)

    share = width // (depth * 4)
    up_first = halve(grad_up.reshape(depth, 2, 2, share, hidden), "x", 1)
    down_first = halve(grad_down.reshape(depth, 2, 2, share, hidden), "y", 2)

    second_part = contract_last(grad_pre, up_full)
    grad_second = second_part[:own_rows] + flip(second_part[own_rows:], "c")
    branch_part = contract_last(act_low, down_full)
    branch = branch_part[:own_rows] + flip(branch_part[own_rows:], "c")
    output = (hidden_sum + branch + b_down.astype(F32)).astype(BF)
    output = output.reshape(groups, block_rows, width)

    grad_y = cot_own.astype(F32)
    grad_hidden = grad_y + norm_back(grad_second, second_scale, second_unit, second_inverse)
    grad_second_gain = jnp.sum(grad_second * second_unit, axis=0)
    grad_second_shift = jnp.sum(grad_second, axis=0)
    grad_attn_own = grad_hidden.astype(BF)
    grad_attn = both(grad_attn_own)
    grad_out = contract_rows(member_out, columns(grad_attn)).astype(BF)
    grad_b_out = jnp.sum(grad_attn_own.astype(F32), axis=0)
    w_out_rows = lax.dynamic_slice_in_dim(w_out, core * half, half, 0)
    grad_member = contract_last(grad_attn, w_out_rows).astype(BF).reshape(rows, heads, HEAD_DIM)
    grad_cent_low = jnp.einsum(
        "hcs,she->hce", member_low, grad_member, preferred_element_type=F32
    ).astype(BF)
    grad_probs = jnp.einsum("hce,she->hcs", grad_cent_low, value_heads, preferred_element_type=F32)
    delta = jnp.sum(probs * grad_probs, axis=-1, keepdims=True)
    grad_scores = (probs * (grad_probs - delta)).astype(BF)
    up_first, down_first, grad_scores = fence((up_first, down_first, grad_scores))
    up_second = halve(joined(up_first), "y", 1)
    down_second = halve(joined(down_first), "x", 1)
    grad_values = (
        jnp.einsum("hcs,hce->she", probs_low, grad_cent_low, preferred_element_type=F32)
        .astype(BF)
        .reshape(rows, half)
    )
    grad_keys = (
        (
            jnp.einsum("hcs,hce->she", grad_scores, centroid_low, preferred_element_type=F32)
            * head_scale
        )
        .astype(BF)
        .reshape(rows, half)
    )
    grad_centroids = (
        jnp.einsum("hcs,she->hce", grad_scores, key_heads, preferred_element_type=F32) * head_scale
    )
    grad_queries = (
        jnp.einsum(
            "hcs,hce->she",
            member_low,
            (grad_centroids / divisor).astype(BF),
            preferred_element_type=F32,
        )
        .astype(BF)
        .reshape(rows, half)
    )
    normed_part = (
        contract_last(grad_queries, wq)
        + contract_last(grad_keys, wk)
        + contract_last(grad_values, wv)
    )
    grad_normed = normed_part[:own_rows] + flip(normed_part[own_rows:], "c")
    squares = [
        contract_rows(normed, grad_queries).astype(BF),
        contract_rows(normed, grad_keys).astype(BF),
        contract_rows(normed, grad_values).astype(BF),
        grad_out,
    ]
    own_unit = first_unit[:own_rows]
    grad_tokens = grad_hidden + norm_back(
        grad_normed, first_scale, own_unit, first_inverse[:own_rows]
    )

    def placed(value, full):
        return lax.dynamic_update_slice_in_dim(
            jnp.zeros((full,), F32), value, core * value.shape[0], 0
        )

    vectors = (
        jnp.sum(grad_normed * own_unit, axis=0),
        jnp.sum(grad_normed, axis=0),
        placed(jnp.sum(grad_queries.astype(F32), axis=0), width),
        placed(jnp.sum(grad_values.astype(F32), axis=0), width),
        grad_b_out,
        grad_second_gain,
        grad_second_shift,
        jnp.sum(grad_y, axis=0),
        placed(grad_b_up, 2 * hidden),
    )
    sizes = [v.shape[0] // (depth * 8) for v in vectors]
    line = 2 * sum(sizes)
    lines = jnp.concatenate([v.reshape(depth, 4, 2, -1) for v in vectors], axis=-1)
    lines = lines.reshape(depth, 2, 2, 1, line).astype(BF)
    lines = jnp.pad(lines, ((0, 0),) * 4 + ((0, 2 * half - line),))
    squares = [jnp.concatenate(squares[2 * i : 2 * i + 2], axis=1) for i in range(2)]
    squares = [v.reshape(depth, 2, 2, share, 2 * half) for v in squares]
    left_first = halve(jnp.concatenate([squares[0], lines], axis=3), "x", 2)
    right_first = halve(squares[1], "y", 1)
    up_second, down_second, left_first, right_first = fence(
        (up_second, down_second, left_first, right_first)
    )
    wide = jnp.concatenate([joined(up_second), joined(down_second)], axis=1)
    wide_sum = over_layers(wide)
    swap = [(y * 2 + c, c * 2 + y) for y in range(2) for c in range(2)]
    wide_sum = lax.ppermute(wide_sum, ("y", "c"), swap)
    grad_w_up = wide_sum[:share]
    grad_w_down = wide_sum[share:].T

    left_second = halve(joined(left_first), "y", 1)
    right_second = halve(joined(right_first), "x", 1)
    blocks = grad_tokens.astype(BF).reshape(groups, block_rows, width)
    back = jnp.concatenate([blocks, output], axis=1)
    left_second, right_second, back = fence((left_second, right_second, back))
    back = in_order(over_chips(lambda step: back[step]))
    grad_tokens = back[:, :block_rows].astype(F32)
    output = back[:, block_rows:]
    total = over_layers(
        jnp.concatenate([joined(left_second), joined(right_second)], axis=1)
    )
    tile = share // 2
    line_sum = total[share, :line].reshape(2, line // 2)
    line_sum = jnp.pad(line_sum, ((0, 0), (0, 2 * half - line // 2)))[:, None]
    squared = jnp.concatenate(
        [
            total[:share].reshape(2, tile, 2 * half),
            total[share + 1 :].reshape(2, tile, 2 * half),
            line_sum,
        ],
        axis=1,
    )
    away = flip(pick(squared, 1 - core), "c")
    kept = pick(squared, core)
    line_own = (kept[2 * tile] + away[2 * tile])[: line // 2]
    kept, away = [v[: 2 * tile].reshape(2, tile, 2, half) for v in (kept, away)]
    full = jnp.where(
        core == 0,
        jnp.concatenate([kept, away], axis=3),
        jnp.concatenate([away, kept], axis=3),
    )
    full = [full[0, :, 0], full[0, :, 1], full[1, :, 0], full[1, :, 1]]
    pieces = []
    place = 0
    for size in sizes:
        pieces.append(line_own[place : place + size])
        place += size
    return (
        output,
        grad_tokens,
        pieces[0],
        pieces[1],
        full[0],
        pieces[2],
        full[1],
        full[2],
        pieces[3],
        full[3],
        pieces[4],
        pieces[5],
        pieces[6],
        grad_w_up,
        pieces[8],
        grad_w_down,
        pieces[7],
    )


def owning(mesh):
    shape = (mesh.shape["dp"], 2, 2, 2)
    split = Mesh(mesh.devices.reshape(shape), ("dp", "y", "x", "c"))
    rows = ("y", "x", "c")
    whole = ("dp", "y", "x", "c")
    return jax.shard_map(
        owned,
        mesh=split,
        in_specs=(
            P("dp", rows, None),
            P("dp", None, rows),
            *(P(),) * 11,
            P(("x", "c"), "y"),
            P("y"),
            P("y", ("x", "c")),
            P(),
            P("dp", rows, None),
        ),
        out_specs=(
            P("dp", rows, None),
            P("dp", rows, None),
            P(whole),
            P(whole),
            P(whole, None),
            P(whole),
            P(whole, None),
            P(whole, None),
            P(whole),
            P(whole, None),
            P(whole),
            P(whole),
            P(whole),
            P(("dp", "x", "c"), "y"),
            P(whole),
            P("y", ("dp", "x", "c")),
            P(whole),
        ),
        check_vma=False,
    )


def solution(mesh):
    def step(tokens, *rest):
        groups = tokens.shape[0] // mesh.shape["dp"]
        fits = mesh.shape["hid"] == 2 and mesh.shape["dm"] == 4 and groups == 4
        return (owning if fits else generic)(mesh)(tokens, *rest)

    return step
```
